256 devices in a mesh: xg: 4 (over x_hi, core), yd: 64 (over x_lo, z, y).
Axes of the slice: x: 4 (x_hi: 2, x_lo: 2; x = x_hi * 2 + x_lo), y: 4, z: 8, core: 2. Of those that a mesh axis runs over, the one named last changes fastest.
Arguments:
- mobile: float32 [4096, 1, 1024], P('yd', None, 'xg'), may hold values from 0 to 2
- dispersion_x: float32 [4096, 1, 1024], P('yd', None, 'xg'), may hold values from 0.5 to 200000
- dispersion_y: float32 [4096, 1, 1024], P('yd', None, 'xg'), may hold values from 0.5 to 200000
- capacity: float32 [4096, 1, 1024], P('yd', None, 'xg'), may hold values from 0.5 to 8
- immobile: float32 [4, 4096, 1, 1024], P(None, 'yd', None, 'xg'), may hold values from 0 to 2
- exchange_rates: float32 [4], replicated, may hold values from 0.02 to 50
- rate_shares: float32 [4], replicated, may hold values from 0.1 to 1
Outputs:
- updated: float32 [4096, 1, 1024], P('yd', None, 'xg')
The draws below stay inside these ranges and needn't reach their ends.
All inputs are finite; a program needn't handle non-finite values.
Results may differ from the reference program's by a relative error of at most 0.0003.
Values sent between devices are 32-bit elements; how exact they have to be, the bound alone decides.
A program may use at most 64 MiB of HBM per device.

```python
import math
import jax
import jax.numpy as jnp
from jax import lax

ZS = 1
RATES = 4
NX = 1024
NY = 4096


def layered_faces(key, line_shape, lowest):
    key_line = jax.random.fold_in(key, 11)
    key_face = jax.random.fold_in(key, 23)
    line_log = jax.random.uniform(key_line, line_shape, jnp.float32, math.log(lowest), 0.0)
    face_log = jax.random.uniform(key_face, (NY, ZS, NX), jnp.float32, -math.log(2.0), math.log(2.0))
    return 100000.0 * jnp.exp(line_log + face_log)


def draw_dispersion_x(key, part):
    lowest = 1e-05
    return layered_faces(key, (NY, ZS, 1), lowest).astype(jnp.float32)


def draw_dispersion_y(key, part):
    lowest = 1e-05
    return layered_faces(key, (1, ZS, NX), lowest).astype(jnp.float32)


def shard_levels(key, shape, cuts, least, top_value):
    def one(position, parts):
        draws = jax.random.uniform(jax.random.fold_in(jax.random.fold_in(key, 6), position), (parts,), jnp.float32, least / len(cuts), top_value / len(cuts))
        return jnp.repeat(jnp.exp(draws), shape[position] // parts).reshape((-1,) + (1,) * (len(shape) - position - 1))

    loudness = one(*cuts[0])
    for cut in cuts[1:]:
        loudness = loudness * one(*cut)
    return loudness


def setup_inputs(seed: int = 0) -> dict:
    splits = jax.random.split(jax.random.key(seed), 8)
    mobile = jnp.clip(2.0 * jax.random.uniform(splits[0], (NY, ZS, NX), jnp.float32) ** shard_levels(splits[0], (NY, ZS, NX), ((0, 64), (2, 4)), -0.2, 0.2), 0.0, 2.0)
    dispersion_x = draw_dispersion_x(jax.random.fold_in(splits[7], 71), 0)
    dispersion_y = draw_dispersion_y(jax.random.fold_in(splits[7], 71), 0)
    capacity = jnp.clip(jnp.exp(math.log(8.0) - 2.7725887 * jax.random.uniform(splits[3], (NY, ZS, NX), jnp.float32) ** shard_levels(splits[3], (NY, ZS, NX), ((0, 64), (2, 4)), -0.2, 0.2)), 0.5, 8.0)
    immobile = jnp.clip(2.0 * jax.random.uniform(splits[4], (RATES, NY, ZS, NX), jnp.float32) ** shard_levels(splits[4], (RATES, NY, ZS, NX), ((1, 64), (3, 4)), -0.2, 0.2), 0.0, 2.0)
    exchange_rates = jnp.clip(jnp.exp(jax.random.uniform(splits[5], (RATES,), jnp.float32, math.log(0.02), math.log(50.0))), 0.02, 50.0)
    rate_shares = jnp.clip(jnp.exp(jax.random.uniform(splits[6], (RATES,), jnp.float32, math.log(0.1), math.log(1.0))), 0.1, 1.0)
    return dict(mobile=mobile, dispersion_x=dispersion_x, dispersion_y=dispersion_y, capacity=capacity, immobile=immobile, exchange_rates=exchange_rates, rate_shares=rate_shares)


def periodic_solve(face_coef, storage, right_side, axis):
    length = right_side.shape[axis]
    sub_coef = -face_coef
    super_coef = -jnp.roll(face_coef, -1, axis)
    main_coef = storage + face_coef - super_coef
    stride = 1
    while stride < length // 2:
        sub_left = jnp.roll(sub_coef, stride, axis)
        main_left = jnp.roll(main_coef, stride, axis)
        super_left = jnp.roll(super_coef, stride, axis)
        side_left = jnp.roll(right_side, stride, axis)
        sub_right = jnp.roll(sub_coef, -stride, axis)
        main_right = jnp.roll(main_coef, -stride, axis)
        super_right = jnp.roll(super_coef, -stride, axis)
        side_right = jnp.roll(right_side, -stride, axis)
        left_ratio = sub_coef / main_left
        right_ratio = super_coef / main_right
        main_coef = main_coef - left_ratio * super_left - right_ratio * sub_right
        right_side = right_side - left_ratio * side_left - right_ratio * side_right
        sub_coef = -left_ratio * sub_left
        super_coef = -right_ratio * super_right
        stride = stride * 2
    coupling = sub_coef + super_coef
    main_other = jnp.roll(main_coef, stride, axis)
    coupling_other = jnp.roll(coupling, stride, axis)
    side_other = jnp.roll(right_side, stride, axis)
    return (right_side * main_other - coupling * side_other) / (main_coef * main_other - coupling * coupling_other)


def reference(mobile, dispersion_x, dispersion_y, capacity, immobile, exchange_rates, rate_shares):
    weights = rate_shares * exchange_rates / (1.0 + exchange_rates)

    def one_plane(inputs):
        plane_mobile, plane_dx, plane_dy, plane_capacity, plane_immobile = inputs
        gain_terms = plane_capacity[None] * weights[:, None, None]
        storage = 1.0 + jnp.sum(gain_terms, axis=0)
        source = plane_mobile + jnp.sum(gain_terms * plane_immobile, axis=0)
        after_x = periodic_solve(plane_dx, storage, source, 1)
        return periodic_solve(plane_dy, storage, storage * after_x, 0)

    planes = lax.map(one_plane, (mobile.transpose(1, 0, 2), dispersion_x.transpose(1, 0, 2), dispersion_y.transpose(1, 0, 2), capacity.transpose(1, 0, 2), immobile.transpose(2, 0, 1, 3)))
    return planes.transpose(1, 0, 2)
```

```python
import functools

import jax
import jax.numpy as jnp
from jax import lax
from jax.experimental import pallas as pl
from jax.experimental.pallas import tpu as pltpu
from jax.sharding import PartitionSpec as P

MESH = pl.DeviceIdType.MESH
Y_SIZE, Z_SIZE, XLO_SIZE, XG_SIZE = 4, 8, 2, 4
PLANE = XLO_SIZE * Y_SIZE
ROWS = 128
LANES = 128
SUB = 8

roll = pltpu.roll


def join_coef(left, right):
    e_a, gl_a, gr_a = left
    e_b, gl_b, gr_b = right
    ground = gr_a + gl_b
    inverse = 1.0 / (ground + (e_a + e_b))
    a = e_a * inverse
    b = e_b * inverse
    return (e_a * b, gl_a + a * ground, gr_b + b * ground), (a, b, inverse)


def join_side(left, right, factors):
    a, b, _ = factors
    middle = left[1] + right[0]
    return (left[0] + a * middle, right[1] + b * middle), middle


def between(factors, middle, u_left, u_right):
    a, b, inverse = factors
    return middle * inverse + a * u_left + b * u_right


def halves(values):
    count = values.shape[0]
    pairs = values.reshape((count // 2, 2) + values.shape[1:])
    return pairs[:, 0], pairs[:, 1]


def woven(first, second):
    count = first.shape[0]
    return jnp.stack([first, second], axis=1).reshape((2 * count,) + first.shape[1:])


def chain_coef(face, ground):
    (e_a, e_b), (g_a, g_b) = halves(face), halves(ground)
    inverse = 1.0 / (g_a + (e_a + e_b))
    a = e_a * inverse
    b = e_b * inverse
    coef = (e_a * b, a * g_a, g_b + b * g_a)
    saved = [(a, b, inverse)]
    while coef[0].shape[0] > 1:
        split = [halves(value) for value in coef]
        coef, factors = join_coef([s[0] for s in split], [s[1] for s in split])
        saved.append(factors)
    return tuple(value[0] for value in coef), saved


def chain_side(source, saved):
    f_a, f_b = halves(source)
    a, b, _ = saved[0]
    side = (a * f_a, f_b + b * f_a)
    middles = [f_a]
    for factors in saved[1:]:
        split = [halves(value) for value in side]
        side, middle = join_side([s[0] for s in split], [s[1] for s in split], factors)
        middles.append(middle)
    return tuple(value[0] for value in side), middles


def chain_back(saved, middles, u_left, u_right):
    u_left, u_right = u_left[None], u_right[None]
    for level in reversed(range(len(saved))):
        u_mid = between(saved[level], middles[level], u_left, u_right)
        if level:
            u_left, u_right = woven(u_left, u_mid), woven(u_mid, u_right)
        else:
            u_right = woven(u_mid, u_right)
    return u_right


def ahead(value, steps):
    return roll(value, value.shape[-2] - steps, value.ndim - 2)


def behind(value, steps):
    return roll(value, steps, value.ndim - 2)


def sub_coef(coef, steps):
    saved = []
    for step in steps:
        coef, factors = join_coef(coef, [ahead(value, step) for value in coef])
        saved.append(factors)
    return coef, saved


def sub_side(side, saved, steps):
    middles = []
    for step, factors in zip(steps, saved):
        side, middle = join_side(side, [ahead(value, step) for value in side], factors)
        middles.append(middle)
    return side, middles


def sub_back(saved, middles, steps, u_left, u_right):
    place = lax.broadcasted_iota(jnp.int32, u_left.shape, u_left.ndim - 2)
    for step, factors, middle in reversed(list(zip(steps, saved, middles))):
        u_mid = between(factors, middle, u_left, u_right)
        first = (place & step) == 0
        u_left, u_right = (
            jnp.where(first, u_left, behind(u_mid, step)),
            jnp.where(first, u_mid, behind(u_right, step)),
        )
    return u_left, u_right


def ring_coef(first, second):
    link = first[0] + second[0]
    ground_q = first[2] + second[1]
    ground_p = second[2] + first[1]
    inverse = 1.0 / (ground_q * ground_p + link * (ground_q + ground_p))
    link = link * inverse
    return link, ground_p * inverse + link, ground_q * inverse + link


def ring_solve(ring, first, second):
    link, to_q, to_p = ring
    f_q = first[1] + second[0]
    f_p = second[1] + first[0]
    return to_p * f_p + link * f_q, to_q * f_q + link * f_p


def strided(ref, stride):
    return jnp.stack([ref[pl.ds(start, SUB, stride=stride), :] for start in range(stride)])


def kernel(
    mobile_hbm, dx_hbm, dy_hbm, cap_hbm, imm_hbm, rates_ref, shares_ref, out_ref,
    mobile_ref, dx_ref, dy_ref, cap_ref, imm_ref, sto_ref, work_ref, work2_ref,
    x_ref, pc_ref, pr_ref, zc_ref, zr_ref, pick_ref,
    in_sem, x_send, x_recv, pc_send, pc_recv, pr_send, pr_recv,
    zc_send, zc_recv, zr_send, zr_recv,
):
    xg = lax.axis_index("xg")
    yd = lax.axis_index("yd")
    xlo = yd // (Z_SIZE * Y_SIZE)
    zz = (yd // Y_SIZE) % Z_SIZE
    yy = yd % Y_SIZE
    slot = xlo * Y_SIZE + yy

    loads = [
        pltpu.make_async_copy(src, dst, in_sem.at[i])
        for i, (src, dst) in enumerate(
            [(imm_hbm, imm_ref), (cap_hbm, cap_ref), (mobile_hbm, mobile_ref), (dx_hbm, dx_ref), (dy_hbm, dy_ref)]
        )
    ]
    for load in loads:
        load.start()

    x_peers = [{"xg": (xg + k) % XG_SIZE, "yd": yd} for k in range(1, XG_SIZE)]
    plane_peers = []
    for k in range(1, PLANE):
        other = (slot + k) % PLANE
        plane_peers.append({"xg": xg, "yd": (other // Y_SIZE) * (Z_SIZE * Y_SIZE) + zz * Y_SIZE + other % Y_SIZE})
    z_peers = [
        {"xg": xg, "yd": xlo * (Z_SIZE * Y_SIZE) + ((zz + k) % Z_SIZE) * Y_SIZE + yy} for k in range(1, Z_SIZE)
    ]
    barrier = pltpu.get_barrier_semaphore()
    for peer in z_peers + plane_peers + x_peers:
        pl.semaphore_signal(barrier, inc=1, device_id=peer, device_id_type=MESH)

    def sends(ref, rows, position, peers, send_sem, recv_sem):
        part = ref.at[pl.ds(pl.multiple_of(position * rows, rows), rows)]
        return [
            pltpu.make_async_remote_copy(
                src_ref=part, dst_ref=part, send_sem=send_sem.at[k], recv_sem=recv_sem.at[k],
                device_id=peer, device_id_type=MESH,
            )
            for k, peer in enumerate(peers)
        ]

    weights = []
    for k in range(4):
        rate = jnp.full((SUB, LANES), rates_ref[k], jnp.float32)
        weights.append(rate * jnp.full((SUB, LANES), shares_ref[k], jnp.float32) / (1.0 + rate))
    loads[0].wait()
    loads[1].wait()
    loads[2].wait()
    capacity = cap_ref[...].reshape(16, SUB, LANES)
    imm = imm_ref[...].reshape(4, 16, SUB, LANES)
    storage = 1.0 + capacity * (weights[0] + weights[1] + weights[2] + weights[3])
    mixed = weights[0] * imm[0] + weights[1] * imm[1] + weights[2] * imm[2] + weights[3] * imm[3]
    source = mobile_ref[...].reshape(16, SUB, LANES) + capacity * mixed
    storage = storage.reshape(ROWS, LANES)
    sto_ref[...] = storage

    loads[3].wait()
    work_ref[...] = jnp.transpose(dx_ref[...])
    work2_ref[...] = jnp.transpose(storage)
    x_coef, x_saved = chain_coef(strided(work_ref, 16), strided(work2_ref, 16))
    work_ref[...] = jnp.transpose(source.reshape(ROWS, LANES))
    x_side, x_mid = chain_side(strided(work_ref, 16), x_saved)
    steps = (1, 2, 4)
    x_coef, xs_saved = sub_coef(x_coef, steps)
    x_side, xs_mid = sub_side(x_side, xs_saved, steps)
    for k, value in enumerate(x_coef + x_side):
        x_ref[0, pl.ds(k, 1), :] = value[0:1]

    loads[4].wait()
    y_face = strided(dy_ref, 16).reshape(8, 2, SUB, LANES)
    y_ground = strided(sto_ref, 16).reshape(8, 2, SUB, LANES)
    y_coef, y_saved = chain_coef(y_face, y_ground)
    y_coef, ys_saved = sub_coef(y_coef, steps)
    base = pl.multiple_of(slot * 8, 8)
    for k in range(3):
        for t in range(2):
            pc_ref[pl.ds(base + 2 * k + t, 1), :] = y_coef[k][t, 0:1]

    pl.semaphore_wait(barrier, len(z_peers + plane_peers + x_peers))

    x_copies = [
        pltpu.make_async_remote_copy(
            src_ref=x_ref.at[0], dst_ref=x_ref.at[XG_SIZE - k], send_sem=x_send.at[k - 1],
            recv_sem=x_recv.at[k - 1], device_id=x_peers[k - 1], device_id_type=MESH,
        )
        for k in range(1, XG_SIZE)
    ]
    for copy in x_copies:
        copy.start()
    pc_copies = sends(pc_ref, 8, slot, plane_peers, pc_send, pc_recv)
    for copy in pc_copies:
        copy.start()

    for copy in x_copies:
        copy.wait()

    def next_lane(value):
        return roll(value, LANES - 1, 1)

    def block(g):
        rows = [x_ref[g, pl.ds(k, 1), :] for k in range(5)]
        rows = [jnp.broadcast_to(row, (SUB, LANES)) for row in rows]
        later = [next_lane(row) for row in rows]
        coef, factors = join_coef(rows[:3], later[:3])
        side, middle = join_side(rows[3:], later[3:], factors)
        return coef, side, factors, middle

    own_coef, own_side, own_factors, own_middle = block(0)
    rest_coef, rest_side, _, _ = block(1)
    for g in (2, 3):
        coef, side, _, _ = block(g)
        rest_coef, factors = join_coef(rest_coef, coef)
        rest_side, _ = join_side(rest_side, side, factors)
    u_before, u_last = ring_solve(ring_coef(own_coef, rest_coef), own_side, rest_side)
    u_half = between(own_factors, own_middle, u_before, u_last)
    even = (lax.broadcasted_iota(jnp.int32, (SUB, LANES), 1) & 1) == 0
    u_left = jnp.where(even, u_before, roll(u_half, 1, 1))
    u_right = jnp.where(even, u_half, roll(u_last, 1, 1))
    u_left, u_right = sub_back(xs_saved, xs_mid, steps, u_left, u_right)
    after_x = chain_back(x_saved, x_mid, u_left, u_right)
    for v in range(16):
        work_ref[pl.ds(v, SUB, stride=16), :] = after_x[v]
    work2_ref[...] = jnp.transpose(work_ref[...]) * sto_ref[...]

    y_side, y_mid = chain_side(strided(work2_ref, 16).reshape(8, 2, SUB, LANES), y_saved)
    y_side, ys_mid = sub_side(y_side, ys_saved, steps)
    for k in range(2):
        for t in range(2):
            pr_ref[pl.ds(base + 2 * k + t, 1), :] = y_side[k][t, 0:1]
    pr_copies = sends(pr_ref, 8, slot, plane_peers, pr_send, pr_recv)
    for copy in pr_copies:
        copy.start()

    for copy in pc_copies:
        copy.wait()

    def plane_rows(ref, k):
        return jnp.stack([ref[pl.ds(2 * k + t, PLANE, stride=8), :] for t in range(2)])

    p_steps = (1, 2)
    p_coef, p_saved = sub_coef([plane_rows(pc_ref, k) for k in range(3)], p_steps)
    z_base = pl.multiple_of(zz * 16, 16)
    for h in range(2):
        for k in range(3):
            for t in range(2):
                zc_ref[pl.ds(z_base + 8 * h + 2 * k + t, 1), :] = p_coef[k][t, 4 * h : 4 * h + 1]
    zc_copies = sends(zc_ref, 16, zz, z_peers, zc_send, zc_recv)
    for copy in zc_copies:
        copy.start()

    for copy in pr_copies:
        copy.wait()
    p_side, p_mid = sub_side([plane_rows(pr_ref, k) for k in range(2)], p_saved, p_steps)
    r_base = pl.multiple_of(zz * 8, 8)
    for h in range(2):
        for k in range(2):
            for t in range(2):
                zr_ref[pl.ds(r_base + 4 * h + 2 * k + t, 1), :] = p_side[k][t, 4 * h : 4 * h + 1]
    zr_copies = sends(zr_ref, 8, zz, z_peers, zr_send, zr_recv)
    for copy in zr_copies:
        copy.start()

    for copy in zc_copies:
        copy.wait()

    def z_rows(ref, stride, half_rows, k):
        return jnp.stack(
            [
                jnp.stack([ref[pl.ds(half_rows * h + 2 * k + t, Z_SIZE, stride=stride), :] for t in range(2)])
                for h in range(2)
            ]
        )

    z_coef, z_saved = sub_coef([z_rows(zc_ref, 16, 8, k) for k in range(3)], steps)
    z_ring = ring_coef([value[0] for value in z_coef], [value[1] for value in z_coef])

    for copy in zr_copies:
        copy.wait()
    z_side, z_mid = sub_side([z_rows(zr_ref, 8, 4, k) for k in range(2)], z_saved, steps)
    u_p, u_q = ring_solve(z_ring, [value[0] for value in z_side], [value[1] for value in z_side])

    def spread(value):
        return jnp.broadcast_to(value[:, 0:1], value.shape)

    def picked(u_left, u_right, place):
        for i, value in enumerate((u_left, u_right)):
            for t in range(2):
                pick_ref[i, t] = value[t]
        return tuple(
            jnp.stack([pick_ref[i, t, pl.ds(place, SUB, stride=0), :] for t in range(2)]) for i in range(2)
        )

    lower = xlo == 0
    u_p, u_q = spread(u_p), spread(u_q)
    u_left, u_right = jnp.where(lower, u_p, u_q), jnp.where(lower, u_q, u_p)
    own_saved = [tuple(jnp.where(lower, value[0], value[1]) for value in factors) for factors in z_saved]
    own_mid = [jnp.where(lower, value[0], value[1]) for value in z_mid]
    u_left, u_right = sub_back(own_saved, own_mid, steps, u_left, u_right)
    u_left, u_right = picked(u_left, u_right, zz)
    u_left, u_right = sub_back(p_saved, p_mid, p_steps, u_left, u_right)
    u_left, u_right = picked(u_left, u_right, slot)
    u_left, u_right = sub_back(ys_saved, ys_mid, steps, u_left, u_right)
    updated = chain_back(y_saved, y_mid, u_left, u_right)
    for v in range(8):
        for t in range(2):
            out_ref[pl.ds(2 * v + t, SUB, stride=16), :] = updated[v, t]


def local(mobile, dispersion_x, dispersion_y, capacity, immobile, exchange_rates, rate_shares):
    flat = [value.reshape(ROWS, LANES) for value in (mobile, dispersion_x, dispersion_y, capacity)]
    any_spec = pl.BlockSpec(memory_space=pl.ANY)
    smem_spec = pl.BlockSpec(memory_space=pltpu.SMEM)
    square = pltpu.VMEM((ROWS, LANES), jnp.float32)
    dma = pltpu.SemaphoreType.DMA
    updated = pl.pallas_call(
        kernel,
        out_shape=jax.ShapeDtypeStruct((ROWS, LANES), jnp.float32),
        in_specs=[any_spec] * 5 + [smem_spec] * 2,
        out_specs=pl.BlockSpec(memory_space=pltpu.VMEM),
        scratch_shapes=[
            square, square, square, square, pltpu.VMEM((4 * ROWS, LANES), jnp.float32), square, square, square,
            pltpu.VMEM((XG_SIZE, 8, LANES), jnp.float32),
            pltpu.VMEM((PLANE * 8, LANES), jnp.float32),
            pltpu.VMEM((PLANE * 8, LANES), jnp.float32),
            pltpu.VMEM((Z_SIZE * 16, LANES), jnp.float32),
            pltpu.VMEM((Z_SIZE * 8, LANES), jnp.float32),
            pltpu.VMEM((2, 2, SUB, LANES), jnp.float32),
            dma((5,)),
            dma((XG_SIZE - 1,)), dma((XG_SIZE - 1,)),
            dma((PLANE - 1,)), dma((PLANE - 1,)), dma((PLANE - 1,)), dma((PLANE - 1,)),
            dma((Z_SIZE - 1,)), dma((Z_SIZE - 1,)), dma((Z_SIZE - 1,)), dma((Z_SIZE - 1,)),
        ],
        compiler_params=pltpu.CompilerParams(collective_id=0, has_side_effects=True),
    )(*flat, immobile.reshape(4 * ROWS, LANES), exchange_rates, rate_shares)
    return updated.reshape(mobile.shape)


def solution(mesh):
    return jax.shard_map(
        local,
        mesh=mesh,
        in_specs=(
            P("yd", None, "xg"),
            P("yd", None, "xg"),
            P("yd", None, "xg"),
            P("yd", None, "xg"),
            P(None, "yd", None, "xg"),
            P(),
            P(),
        ),
        out_specs=P("yd", None, "xg"),
        check_vma=False,
    )
```

```python
import functools

import jax
import jax.numpy as jnp
from jax import lax
from jax.experimental import pallas as pl
from jax.experimental.pallas import tpu as pltpu
from jax.sharding import PartitionSpec as P

MESH = pl.DeviceIdType.MESH
Y_SIZE, Z_SIZE, XLO_SIZE, XG_SIZE = 4, 8, 2, 4
PLANE = XLO_SIZE * Y_SIZE
ROWS = 128
LANES = 128
SUB = 8

roll = pltpu.roll


def join_coef(left, right):
    e_a, gl_a, gr_a = left
    e_b, gl_b, gr_b = right
    ground = gr_a + gl_b
    inverse = 1.0 / (ground + (e_a + e_b))
    a = e_a * inverse
    b = e_b * inverse
    return (e_a * b, gl_a + a * ground, gr_b + b * ground), (a, b, inverse)


def join_side(left, right, factors):
    a, b, _ = factors
    middle = left[1] + right[0]
    return (left[0] + a * middle, right[1] + b * middle), middle


def between(factors, middle, u_left, u_right):
    a, b, inverse = factors
    return middle * inverse + a * u_left + b * u_right


def halves(values):
    count = values.shape[0]
    pairs = values.reshape((count // 2, 2) + values.shape[1:])
    return pairs[:, 0], pairs[:, 1]


def woven(first, second):
    count = first.shape[0]
    return jnp.stack([first, second], axis=1).reshape((2 * count,) + first.shape[1:])


def chain_coef(face, ground):
    (e_a, e_b), (g_a, g_b) = halves(face), halves(ground)
    inverse = 1.0 / (g_a + (e_a + e_b))
    a = e_a * inverse
    b = e_b * inverse
    coef = (e_a * b, a * g_a, g_b + b * g_a)
    saved = [(a, b, inverse)]
    while coef[0].shape[0] > 1:
        split = [halves(value) for value in coef]
        coef, factors = join_coef([s[0] for s in split], [s[1] for s in split])
        saved.append(factors)
    return tuple(value[0] for value in coef), saved


def chain_side(source, saved):
    f_a, f_b = halves(source)
    a, b, _ = saved[0]
    side = (a * f_a, f_b + b * f_a)
    middles = [f_a]
    for factors in saved[1:]:
        split = [halves(value) for value in side]
        side, middle = join_side([s[0] for s in split], [s[1] for s in split], factors)
        middles.append(middle)
    return tuple(value[0] for value in side), middles


def chain_back(saved, middles, u_left, u_right):
    u_left, u_right = u_left[None], u_right[None]
    for level in reversed(range(len(saved))):
        u_mid = between(saved[level], middles[level], u_left, u_right)
        if level:
            u_left, u_right = woven(u_left, u_mid), woven(u_mid, u_right)
        else:
            u_right = woven(u_mid, u_right)
    return u_right


def ahead(value, steps):
    return roll(value, value.shape[-2] - steps, value.ndim - 2)


def behind(value, steps):
    return roll(value, steps, value.ndim - 2)


def sub_coef(coef, steps):
    saved = []
    for step in steps:
        coef, factors = join_coef(coef, [ahead(value, step) for value in coef])
        saved.append(factors)
    return coef, saved


def sub_side(side, saved, steps):
    middles = []
    for step, factors in zip(steps, saved):
        side, middle = join_side(side, [ahead(value, step) for value in side], factors)
        middles.append(middle)
    return side, middles


def sub_back(saved, middles, steps, u_left, u_right):
    place = lax.broadcasted_iota(jnp.int32, u_left.shape, u_left.ndim - 2)
    for step, factors, middle in reversed(list(zip(steps, saved, middles))):
        u_mid = between(factors, middle, u_left, u_right)
        first = (place & step) == 0
        u_left, u_right = (
            jnp.where(first, u_left, behind(u_mid, step)),
            jnp.where(first, u_mid, behind(u_right, step)),
        )
    return u_left, u_right


def ring_coef(first, second):
    link = first[0] + second[0]
    ground_q = first[2] + second[1]
    ground_p = second[2] + first[1]
    inverse = 1.0 / (ground_q * ground_p + link * (ground_q + ground_p))
    link = link * inverse
    return link, ground_p * inverse + link, ground_q * inverse + link


def ring_solve(ring, first, second):
    link, to_q, to_p = ring
    f_q = first[1] + second[0]
    f_p = second[1] + first[0]
    return to_p * f_p + link * f_q, to_q * f_q + link * f_p


def strided(ref, stride):
    return jnp.stack([ref[pl.ds(start, SUB, stride=stride), :] for start in range(stride)])


def kernel(
    mobile_hbm, dx_hbm, dy_hbm, cap_hbm, imm_hbm, rates_hbm, shares_hbm, out_ref,
    mobile_ref, dx_ref, dy_ref, cap_ref, imm_ref, rates_ref, shares_ref, sto_ref, work_ref, work2_ref,
    x_ref, pc_ref, pr_ref, zc_ref, part_ref, parts_ref, sums_ref, pick_ref,
    in_sem, x_send, x_recv, pc_send, pc_recv, pr_send, pr_recv,
    zc_send, zc_recv, part_send, part_recv, ready,
):
    xg = lax.axis_index("xg")
    yd = lax.axis_index("yd")
    xlo = yd // (Z_SIZE * Y_SIZE)
    zz = (yd // Y_SIZE) % Z_SIZE
    yy = yd % Y_SIZE
    slot = xlo * Y_SIZE + yy

    loads = [
        pltpu.make_async_copy(src, dst, in_sem.at[i])
        for i, (src, dst) in enumerate(
            [
                (rates_hbm, rates_ref), (shares_hbm, shares_ref), (cap_hbm, cap_ref), (dy_hbm, dy_ref),
                (dx_hbm, dx_ref), (imm_hbm, imm_ref), (mobile_hbm, mobile_ref),
            ]
        )
    ]
    for load in loads:
        load.start()

    x_peers = [{"xg": (xg + k) % XG_SIZE, "yd": yd} for k in range(1, XG_SIZE)]
    plane_peers = []
    for k in range(1, PLANE):
        other = (slot + k) % PLANE
        plane_peers.append({"xg": xg, "yd": (other // Y_SIZE) * (Z_SIZE * Y_SIZE) + zz * Y_SIZE + other % Y_SIZE})
    plane_starts = [((zz + k) % Z_SIZE) * Y_SIZE for k in (4, 3, 5, 2, 6, 1, 7)]
    z_peers = [{"xg": xg, "yd": xlo * (Z_SIZE * Y_SIZE) + start + yy} for start in plane_starts]
    barrier = pltpu.get_barrier_semaphore()
    for peer in z_peers + plane_peers + x_peers:
        pl.semaphore_signal(barrier, inc=1, device_id=peer, device_id_type=MESH)

    def sends(ref, position, peers, send_sem, recv_sem):
        part = ref.at[position]
        return [
            pltpu.make_async_remote_copy(
                src_ref=part, dst_ref=part, send_sem=send_sem.at[k], recv_sem=recv_sem.at[k],
                device_id=peer, device_id_type=MESH,
            )
            for k, peer in enumerate(peers)
        ]

    loads[0].wait()
    loads[1].wait()
    weights = []
    for k in range(4):
        rate = jnp.full((SUB, LANES), rates_ref[k], jnp.float32)
        weights.append(rate * jnp.full((SUB, LANES), shares_ref[k], jnp.float32) / (1.0 + rate))
    loads[2].wait()
    capacity = cap_ref[...].reshape(16, SUB, LANES)
    storage = 1.0 + capacity * (weights[0] + weights[1] + weights[2] + weights[3])
    storage = storage.reshape(ROWS, LANES)
    sto_ref[...] = storage

    steps = (1, 2, 4)
    loads[3].wait()
    y_face = strided(dy_ref, 16).reshape(8, 2, SUB, LANES)
    y_ground = strided(sto_ref, 16).reshape(8, 2, SUB, LANES)
    y_coef, y_saved = chain_coef(y_face, y_ground)
    y_coef, ys_saved = sub_coef(y_coef, steps)
    for k in range(3):
        for t in range(2):
            pc_ref[slot, pl.ds(2 * k + t, 1), :] = y_coef[k][t, 0:1]

    loads[4].wait()
    work_ref[...] = jnp.transpose(dx_ref[...])
    work2_ref[...] = jnp.transpose(storage)
    x_coef, x_saved = chain_coef(strided(work_ref, 16), strided(work2_ref, 16))
    loads[5].wait()
    loads[6].wait()
    imm = imm_ref[...].reshape(4, 16, SUB, LANES)
    mixed = weights[0] * imm[0] + weights[1] * imm[1] + weights[2] * imm[2] + weights[3] * imm[3]
    source = mobile_ref[...].reshape(16, SUB, LANES) + capacity * mixed
    work_ref[...] = jnp.transpose(source.reshape(ROWS, LANES))
    x_side, x_mid = chain_side(strided(work_ref, 16), x_saved)
    x_coef, xs_saved = sub_coef(x_coef, steps)
    x_side, xs_mid = sub_side(x_side, xs_saved, steps)
    for k, value in enumerate(x_coef + x_side):
        x_ref[0, pl.ds(k, 1), :] = value[0:1]

    pl.semaphore_wait(barrier, len(z_peers + plane_peers + x_peers))

    x_copies = [
        pltpu.make_async_remote_copy(
            src_ref=x_ref.at[0], dst_ref=x_ref.at[XG_SIZE - k], send_sem=x_send.at[k - 1],
            recv_sem=x_recv.at[k - 1], device_id=x_peers[k - 1], device_id_type=MESH,
        )
        for k in range(1, XG_SIZE)
    ]
    pc_copies = sends(pc_ref, slot, plane_peers, pc_send, pc_recv)
    for copy in x_copies + pc_copies:
        copy.start()
    for peer in z_peers:
        pl.semaphore_signal(ready, inc=1, device_id=peer, device_id_type=MESH)

    for copy in x_copies:
        copy.wait_recv()

    def next_lane(value):
        return roll(value, LANES - 1, 1)

    def block(g):
        rows = [x_ref[g, pl.ds(k, 1), :] for k in range(5)]
        rows = [jnp.broadcast_to(row, (SUB, LANES)) for row in rows]
        later = [next_lane(row) for row in rows]
        coef, factors = join_coef(rows[:3], later[:3])
        side, middle = join_side(rows[3:], later[3:], factors)
        return coef, side, factors, middle

    own_coef, own_side, own_factors, own_middle = block(0)
    rest_coef, rest_side, _, _ = block(1)
    for g in (2, 3):
        coef, side, _, _ = block(g)
        rest_coef, factors = join_coef(rest_coef, coef)
        rest_side, _ = join_side(rest_side, side, factors)
    u_before, u_last = ring_solve(ring_coef(own_coef, rest_coef), own_side, rest_side)
    u_half = between(own_factors, own_middle, u_before, u_last)
    even = (lax.broadcasted_iota(jnp.int32, (SUB, LANES), 1) & 1) == 0
    u_left = jnp.where(even, u_before, roll(u_half, 1, 1))
    u_right = jnp.where(even, u_half, roll(u_last, 1, 1))
    u_left, u_right = sub_back(xs_saved, xs_mid, steps, u_left, u_right)
    after_x = chain_back(x_saved, x_mid, u_left, u_right)
    for v in range(16):
        work_ref[pl.ds(v, SUB, stride=16), :] = after_x[v]
    work2_ref[...] = jnp.transpose(work_ref[...]) * sto_ref[...]

    y_side, y_mid = chain_side(strided(work2_ref, 16).reshape(8, 2, SUB, LANES), y_saved)
    y_side, ys_mid = sub_side(y_side, ys_saved, steps)
    for k in range(2):
        for t in range(2):
            pr_ref[slot, pl.ds(2 * k + t, 1), :] = y_side[k][t, 0:1]
    pr_copies = sends(pr_ref, slot, plane_peers, pr_send, pr_recv)
    for copy in pr_copies:
        copy.start()

    for copy in pc_copies:
        copy.wait_recv()

    def plane_rows(ref, k):
        flat = ref.reshape(PLANE * 8, LANES)
        return jnp.stack([flat[pl.ds(2 * k + t, PLANE, stride=8), :] for t in range(2)])

    def at_row(value, place):
        for t in range(2):
            pick_ref[t] = value[t]
        return jnp.stack([pick_ref[t, pl.ds(place, SUB, stride=0), :] for t in range(2)])

    p_steps = (1, 2)
    p_coef, p_saved = sub_coef([plane_rows(pc_ref, k) for k in range(3)], p_steps)
    for h in range(2):
        for k in range(3):
            for t in range(2):
                zc_ref[zz, pl.ds(8 * h + 2 * k + t, 1), :] = p_coef[k][t, 4 * h : 4 * h + 1]
    zc_copies = sends(zc_ref, zz, z_peers, zc_send, zc_recv)
    for copy in zc_copies:
        copy.start()

    place = lax.broadcasted_iota(jnp.int32, (2, SUB, LANES), 1)
    unit = jnp.where(place == slot, 1.0, 0.0)
    zero = jnp.zeros_like(unit)
    from_left, _ = sub_side((unit, zero), p_saved, p_steps)
    from_right, _ = sub_side((zero, unit), p_saved, p_steps)
    group = xlo * Y_SIZE
    for k in range(2):
        value = at_row(from_left[k], group) * y_side[0] + at_row(from_right[k], group) * y_side[1]
        for t in range(2):
            part_ref[pl.ds(2 * k + t, 1), :] = value[t, 0:1]
    pl.semaphore_wait(ready, len(z_peers))
    part_copies = [
        pltpu.make_async_remote_copy(
            src_ref=part_ref, dst_ref=parts_ref.at[yd], send_sem=part_send, recv_sem=part_recv,
            device_id={"xg": xg, "yd": h * (Z_SIZE * Y_SIZE) + start + y}, device_id_type=MESH,
        )
        for start in plane_starts
        for h in range(XLO_SIZE)
        for y in range(Y_SIZE)
    ]
    for copy in part_copies:
        copy.start()
    for h in range(XLO_SIZE):
        parts_ref[pl.ds(h * (Z_SIZE * Y_SIZE) + zz * Y_SIZE, Y_SIZE)] = jnp.zeros((Y_SIZE, 4, LANES), jnp.float32)

    for copy in zc_copies:
        copy.wait_recv()

    def z_rows(ref, k):
        width = ref.shape[1]
        flat = ref.reshape(Z_SIZE * width, LANES)
        return jnp.stack(
            [
                jnp.stack([flat[pl.ds(width // 2 * h + 2 * k + t, Z_SIZE, stride=width), :] for t in range(2)])
                for h in range(2)
            ]
        )

    z_coef, z_saved = sub_coef([z_rows(zc_ref, k) for k in range(3)], steps)
    z_ring = ring_coef([value[0] for value in z_coef], [value[1] for value in z_coef])

    for copy in pr_copies:
        copy.wait_recv()
    p_side, p_mid = sub_side([plane_rows(pr_ref, k) for k in range(2)], p_saved, p_steps)

    others = parts_ref.at[pl.ds(0, len(part_copies))]
    pltpu.make_async_copy(others, others, part_recv).wait()
    for h in range(2):
        for z in range(Z_SIZE):
            first = h * (Z_SIZE * Y_SIZE) + z * Y_SIZE
            total = parts_ref[first] + parts_ref[first + 1] + (parts_ref[first + 2] + parts_ref[first + 3])
            sums_ref[z, 4 * h : 4 * h + 4, :] = total
    for h in range(2):
        for k in range(2):
            for t in range(2):
                sums_ref[zz, pl.ds(4 * h + 2 * k + t, 1), :] = p_side[k][t, 4 * h : 4 * h + 1]
    z_side, z_mid = sub_side([z_rows(sums_ref, k) for k in range(2)], z_saved, steps)
    u_p, u_q = ring_solve(z_ring, [value[0] for value in z_side], [value[1] for value in z_side])

    def spread(value):
        return jnp.broadcast_to(value[:, 0:1], value.shape)

    lower = xlo == 0
    u_p, u_q = spread(u_p), spread(u_q)
    u_left, u_right = jnp.where(lower, u_p, u_q), jnp.where(lower, u_q, u_p)
    own_saved = [tuple(jnp.where(lower, value[0], value[1]) for value in factors) for factors in z_saved]
    own_mid = [jnp.where(lower, value[0], value[1]) for value in z_mid]
    u_left, u_right = sub_back(own_saved, own_mid, steps, u_left, u_right)
    u_left, u_right = at_row(u_left, zz), at_row(u_right, zz)
    u_left, u_right = sub_back(p_saved, p_mid, p_steps, u_left, u_right)
    u_left, u_right = at_row(u_left, slot), at_row(u_right, slot)
    u_left, u_right = sub_back(ys_saved, ys_mid, steps, u_left, u_right)
    updated = chain_back(y_saved, y_mid, u_left, u_right)
    for v in range(8):
        for t in range(2):
            out_ref[pl.ds(2 * v + t, SUB, stride=16), :] = updated[v, t]

    for copy in x_copies + pc_copies + pr_copies + zc_copies:
        copy.wait_send()
    pltpu.make_async_copy(others, others, part_send).wait()


def local(mobile, dispersion_x, dispersion_y, capacity, immobile, exchange_rates, rate_shares):
    flat = [value.reshape(ROWS, LANES) for value in (mobile, dispersion_x, dispersion_y, capacity)]
    any_spec = pl.BlockSpec(memory_space=pl.ANY)
    square = pltpu.VMEM((ROWS, LANES), jnp.float32)
    zones = pltpu.SMEM((4,), jnp.float32)
    dma = pltpu.SemaphoreType.DMA
    updated = pl.pallas_call(
        kernel,
        out_shape=jax.ShapeDtypeStruct((ROWS, LANES), jnp.float32),
        in_specs=[any_spec] * 7,
        out_specs=pl.BlockSpec(memory_space=pltpu.VMEM),
        scratch_shapes=[
            square, square, square, square, pltpu.VMEM((4 * ROWS, LANES), jnp.float32), zones, zones,
            square, square, square,
            pltpu.VMEM((XG_SIZE, 8, LANES), jnp.float32),
            pltpu.VMEM((PLANE, 8, LANES), jnp.float32),
            pltpu.VMEM((PLANE, 8, LANES), jnp.float32),
            pltpu.VMEM((Z_SIZE, 16, LANES), jnp.float32),
            pltpu.VMEM((4, LANES), jnp.float32),
            pltpu.VMEM((PLANE * Z_SIZE, 4, LANES), jnp.float32),
            pltpu.VMEM((Z_SIZE, 8, LANES), jnp.float32),
            pltpu.VMEM((2, SUB, LANES), jnp.float32),
            dma((7,)),
            dma((XG_SIZE - 1,)), dma((XG_SIZE - 1,)),
            dma((PLANE - 1,)), dma((PLANE - 1,)), dma((PLANE - 1,)), dma((PLANE - 1,)),
            dma((Z_SIZE - 1,)), dma((Z_SIZE - 1,)), dma(()), dma(()),
            pltpu.SemaphoreType.REGULAR,
        ],
        compiler_params=pltpu.CompilerParams(collective_id=0, has_side_effects=True),
    )(*flat, immobile.reshape(4 * ROWS, LANES), exchange_rates, rate_shares)
    return updated.reshape(mobile.shape)


def solution(mesh):
    return jax.shard_map(
        local,
        mesh=mesh,
        in_specs=(
            P("yd", None, "xg"),
            P("yd", None, "xg"),
            P("yd", None, "xg"),
            P("yd", None, "xg"),
            P(None, "yd", None, "xg"),
            P(),
            P(),
        ),
        out_specs=P("yd", None, "xg"),
        check_vma=False,
    )
```

```python
import functools

import jax
import jax.numpy as jnp
from jax import lax
from jax.experimental import pallas as pl
from jax.experimental.pallas import tpu as pltpu
from jax.sharding import PartitionSpec as P

MESH = pl.DeviceIdType.MESH
Y_SIZE, Z_SIZE, XLO_SIZE, XG_SIZE = 4, 8, 2, 4
PLANE = XLO_SIZE * Y_SIZE
ROWS = 128
LANES = 128
SUB = 8

roll = pltpu.roll


def join_coef(left, right):
    e_a, gl_a, gr_a = left
    e_b, gl_b, gr_b = right
    ground = gr_a + gl_b
    inverse = 1.0 / (ground + (e_a + e_b))
    a = e_a * inverse
    b = e_b * inverse
    return (e_a * b, gl_a + a * ground, gr_b + b * ground), (a, b, inverse)


def join_side(left, right, factors):
    a, b, _ = factors
    middle = left[1] + right[0]
    return (left[0] + a * middle, right[1] + b * middle), middle


def between(factors, middle, u_left, u_right):
    a, b, inverse = factors
    return middle * inverse + a * u_left + b * u_right


def halves(values):
    count = values.shape[0]
    pairs = values.reshape((count // 2, 2) + values.shape[1:])
    return pairs[:, 0], pairs[:, 1]


def woven(first, second):
    count = first.shape[0]
    return jnp.stack([first, second], axis=1).reshape((2 * count,) + first.shape[1:])


def chain_coef(face, ground):
    (e_a, e_b), (g_a, g_b) = halves(face), halves(ground)
    inverse = 1.0 / (g_a + (e_a + e_b))
    a = e_a * inverse
    b = e_b * inverse
    coef = (e_a * b, a * g_a, g_b + b * g_a)
    saved = [(a, b, inverse)]
    while coef[0].shape[0] > 1:
        split = [halves(value) for value in coef]
        coef, factors = join_coef([s[0] for s in split], [s[1] for s in split])
        saved.append(factors)
    return tuple(value[0] for value in coef), saved


def chain_side(source, saved):
    f_a, f_b = halves(source)
    a, b, _ = saved[0]
    side = (a * f_a, f_b + b * f_a)
    middles = [f_a]
    for factors in saved[1:]:
        split = [halves(value) for value in side]
        side, middle = join_side([s[0] for s in split], [s[1] for s in split], factors)
        middles.append(middle)
    return tuple(value[0] for value in side), middles


def chain_back(saved, middles, u_left, u_right):
    u_left, u_right = u_left[None], u_right[None]
    for level in reversed(range(len(saved))):
        u_mid = between(saved[level], middles[level], u_left, u_right)
        if level:
            u_left, u_right = woven(u_left, u_mid), woven(u_mid, u_right)
        else:
            u_right = woven(u_mid, u_right)
    return u_right


def ahead(value, steps):
    return roll(value, value.shape[-2] - steps, value.ndim - 2)


def behind(value, steps):
    return roll(value, steps, value.ndim - 2)


def sub_coef(coef, steps):
    saved = []
    for step in steps:
        coef, factors = join_coef(coef, [ahead(value, step) for value in coef])
        saved.append(factors)
    return coef, saved


def sub_side(side, saved, steps):
    middles = []
    for step, factors in zip(steps, saved):
        side, middle = join_side(side, [ahead(value, step) for value in side], factors)
        middles.append(middle)
    return side, middles


def sub_back(saved, middles, steps, u_left, u_right):
    place = lax.broadcasted_iota(jnp.int32, u_left.shape, u_left.ndim - 2)
    for step, factors, middle in reversed(list(zip(steps, saved, middles))):
        u_mid = between(factors, middle, u_left, u_right)
        first = (place & step) == 0
        u_left, u_right = (
            jnp.where(first, u_left, behind(u_mid, step)),
            jnp.where(first, u_mid, behind(u_right, step)),
        )
    return u_left, u_right


def ring_coef(first, second):
    link = first[0] + second[0]
    ground_q = first[2] + second[1]
    ground_p = second[2] + first[1]
    inverse = 1.0 / (ground_q * ground_p + link * (ground_q + ground_p))
    link = link * inverse
    return link, ground_p * inverse + link, ground_q * inverse + link


def ring_solve(ring, first, second):
    link, to_q, to_p = ring
    f_q = first[1] + second[0]
    f_p = second[1] + first[0]
    return to_p * f_p + link * f_q, to_q * f_q + link * f_p


def strided(ref, stride):
    return jnp.stack([ref[pl.ds(start, SUB, stride=stride), :] for start in range(stride)])


def kernel(
    mobile_hbm, dx_hbm, dy_hbm, cap_hbm, imm_hbm, rates_hbm, shares_hbm, out_ref,
    mobile_ref, dx_ref, dy_ref, cap_ref, imm_ref, rates_ref, shares_ref, sto_ref, work_ref, work2_ref,
    x_ref, pc_ref, pr_ref, zc_ref, part_ref, parts_ref, sums_ref, pick_ref,
    in_sem, x_send, x_recv, pc_send, pc_recv, pr_send, pr_recv,
    zc_send, zc_recv, part_send, part_recv, ready,
):
    xg = lax.axis_index("xg")
    yd = lax.axis_index("yd")
    xlo = yd // (Z_SIZE * Y_SIZE)
    zz = (yd // Y_SIZE) % Z_SIZE
    yy = yd % Y_SIZE
    slot = xlo * Y_SIZE + yy

    loads = [
        pltpu.make_async_copy(src, dst, in_sem.at[i])
        for i, (src, dst) in enumerate(
            [
                (rates_hbm, rates_ref), (shares_hbm, shares_ref), (cap_hbm, cap_ref), (dy_hbm, dy_ref),
                (dx_hbm, dx_ref), (imm_hbm, imm_ref), (mobile_hbm, mobile_ref),
            ]
        )
    ]
    for load in loads:
        load.start()

    x_peers = [{"xg": (xg + k) % XG_SIZE, "yd": yd} for k in range(1, XG_SIZE)]
    plane_peers = []
    for k in range(1, PLANE):
        other = (slot + k) % PLANE
        plane_peers.append({"xg": xg, "yd": (other // Y_SIZE) * (Z_SIZE * Y_SIZE) + zz * Y_SIZE + other % Y_SIZE})
    z_peers = [
        {"xg": xg, "yd": xlo * (Z_SIZE * Y_SIZE) + ((zz + k) % Z_SIZE) * Y_SIZE + yy} for k in range(1, Z_SIZE)
    ]
    y_peers = [{"xg": xg, "yd": yd - yy + (yy + k) % Y_SIZE} for k in range(1, Y_SIZE)]
    column = zz * XLO_SIZE + xlo
    starts = []
    for k in range(XLO_SIZE * Z_SIZE - 1):
        other = jnp.where(column <= k, k + 1, k)
        starts.append((other % XLO_SIZE) * (Z_SIZE * Y_SIZE) + (other // XLO_SIZE) * Y_SIZE)
    barrier = pltpu.get_barrier_semaphore()
    for peer in z_peers + plane_peers + x_peers:
        pl.semaphore_signal(barrier, inc=1, device_id=peer, device_id_type=MESH)

    pc_ref[Y_SIZE:] = jnp.ones((Y_SIZE, 8, LANES), jnp.float32)
    pr_ref[Y_SIZE:] = jnp.zeros((Y_SIZE, 8, LANES), jnp.float32)

    def sends(ref, position, peers, send_sem, recv_sem):
        part = ref.at[position]
        return [
            pltpu.make_async_remote_copy(
                src_ref=part, dst_ref=part, send_sem=send_sem.at[k], recv_sem=recv_sem.at[k],
                device_id=peer, device_id_type=MESH,
            )
            for k, peer in enumerate(peers)
        ]

    loads[0].wait()
    loads[1].wait()
    weights = []
    for k in range(4):
        rate = jnp.full((SUB, LANES), rates_ref[k], jnp.float32)
        weights.append(rate * jnp.full((SUB, LANES), shares_ref[k], jnp.float32) / (1.0 + rate))
    loads[2].wait()
    capacity = cap_ref[...].reshape(16, SUB, LANES)
    storage = 1.0 + capacity * (weights[0] + weights[1] + weights[2] + weights[3])
    storage = storage.reshape(ROWS, LANES)
    sto_ref[...] = storage

    steps = (1, 2, 4)
    loads[3].wait()
    y_face = strided(dy_ref, 16).reshape(8, 2, SUB, LANES)
    y_ground = strided(sto_ref, 16).reshape(8, 2, SUB, LANES)
    y_coef, y_saved = chain_coef(y_face, y_ground)
    y_coef, ys_saved = sub_coef(y_coef, steps)
    for k in range(3):
        for t in range(2):
            pc_ref[yy, pl.ds(2 * k + t, 1), :] = y_coef[k][t, 0:1]

    loads[4].wait()
    work_ref[...] = jnp.transpose(dx_ref[...])
    work2_ref[...] = jnp.transpose(storage)
    x_coef, x_saved = chain_coef(strided(work_ref, 16), strided(work2_ref, 16))
    loads[5].wait()
    loads[6].wait()
    imm = imm_ref[...].reshape(4, 16, SUB, LANES)
    mixed = weights[0] * imm[0] + weights[1] * imm[1] + weights[2] * imm[2] + weights[3] * imm[3]
    source = mobile_ref[...].reshape(16, SUB, LANES) + capacity * mixed
    work_ref[...] = jnp.transpose(source.reshape(ROWS, LANES))
    x_side, x_mid = chain_side(strided(work_ref, 16), x_saved)
    x_coef, xs_saved = sub_coef(x_coef, steps)
    x_side, xs_mid = sub_side(x_side, xs_saved, steps)
    for k, value in enumerate(x_coef + x_side):
        x_ref[0, pl.ds(k, 1), :] = value[0:1]

    pl.semaphore_wait(barrier, len(z_peers + plane_peers + x_peers))

    x_copies = [
        pltpu.make_async_remote_copy(
            src_ref=x_ref.at[0], dst_ref=x_ref.at[XG_SIZE - k], send_sem=x_send.at[k - 1],
            recv_sem=x_recv.at[k - 1], device_id=x_peers[k - 1], device_id_type=MESH,
        )
        for k in range(1, XG_SIZE)
    ]
    pc_copies = sends(pc_ref, yy, y_peers, pc_send, pc_recv)
    for copy in x_copies + pc_copies:
        copy.start()
    for peer in z_peers:
        pl.semaphore_signal(ready, inc=1, device_id=peer, device_id_type=MESH)

    for copy in pc_copies:
        copy.wait_recv()

    def group_rows(ref, k):
        flat = ref.reshape(SUB * 8, LANES)
        return jnp.stack([flat[pl.ds(2 * k + t, SUB, stride=8), :] for t in range(2)])

    def spread(value):
        return jnp.broadcast_to(value[:, 0:1], value.shape)

    def at_row(value, place):
        for t in range(2):
            pick_ref[t] = value[t]
        return jnp.stack([pick_ref[t, pl.ds(place, SUB, stride=0), :] for t in range(2)])

    p_steps = (1, 2)
    p_coef, p_saved = sub_coef([group_rows(pc_ref, k) for k in range(3)], p_steps)
    own = xlo * Z_SIZE + zz
    for k in range(3):
        for t in range(2):
            zc_ref[own, pl.ds(2 * k + t, 1), :] = p_coef[k][t, 0:1]
    pl.semaphore_wait(ready, len(z_peers))
    zc_part = zc_ref.at[own, pl.ds(0, 6)]
    zc_copies = [
        pltpu.make_async_remote_copy(
            src_ref=zc_part, dst_ref=zc_part, send_sem=zc_send, recv_sem=zc_recv,
            device_id={"xg": xg, "yd": start + yy}, device_id_type=MESH,
        )
        for start in starts
    ]
    for copy in zc_copies:
        copy.start()

    place = lax.broadcasted_iota(jnp.int32, (2, SUB, LANES), 1)
    unit = jnp.where(place == yy, 1.0, 0.0)
    zero = jnp.zeros_like(unit)
    from_left, _ = sub_side((unit, zero), p_saved, p_steps)
    from_right, _ = sub_side((zero, unit), p_saved, p_steps)
    from_left = [spread(value) for value in from_left]
    from_right = [spread(value) for value in from_right]

    for copy in x_copies:
        copy.wait_recv()

    def next_lane(value):
        return roll(value, LANES - 1, 1)

    def block(g):
        rows = [x_ref[g, pl.ds(k, 1), :] for k in range(5)]
        rows = [jnp.broadcast_to(row, (SUB, LANES)) for row in rows]
        later = [next_lane(row) for row in rows]
        coef, factors = join_coef(rows[:3], later[:3])
        side, middle = join_side(rows[3:], later[3:], factors)
        return coef, side, factors, middle

    own_coef, own_side, own_factors, own_middle = block(0)
    rest_coef, rest_side, _, _ = block(1)
    for g in (2, 3):
        coef, side, _, _ = block(g)
        rest_coef, factors = join_coef(rest_coef, coef)
        rest_side, _ = join_side(rest_side, side, factors)
    u_before, u_last = ring_solve(ring_coef(own_coef, rest_coef), own_side, rest_side)
    u_half = between(own_factors, own_middle, u_before, u_last)
    even = (lax.broadcasted_iota(jnp.int32, (SUB, LANES), 1) & 1) == 0
    u_left = jnp.where(even, u_before, roll(u_half, 1, 1))
    u_right = jnp.where(even, u_half, roll(u_last, 1, 1))
    u_left, u_right = sub_back(xs_saved, xs_mid, steps, u_left, u_right)
    after_x = chain_back(x_saved, x_mid, u_left, u_right)
    for v in range(16):
        work_ref[pl.ds(v, SUB, stride=16), :] = after_x[v]
    work2_ref[...] = jnp.transpose(work_ref[...]) * sto_ref[...]

    y_side, y_mid = chain_side(strided(work2_ref, 16).reshape(8, 2, SUB, LANES), y_saved)
    y_side, ys_mid = sub_side(y_side, ys_saved, steps)
    for k in range(2):
        for t in range(2):
            pr_ref[yy, pl.ds(2 * k + t, 1), :] = y_side[k][t, 0:1]
    pr_copies = sends(pr_ref, yy, y_peers, pr_send, pr_recv)

    for k in range(2):
        value = from_left[k] * y_side[0] + from_right[k] * y_side[1]
        for t in range(2):
            part_ref[pl.ds(2 * k + t, 1), :] = value[t, 0:1]
    part_copies = [
        pltpu.make_async_remote_copy(
            src_ref=part_ref, dst_ref=parts_ref.at[yd], send_sem=part_send, recv_sem=part_recv,
            device_id={"xg": xg, "yd": start + y}, device_id_type=MESH,
        )
        for start in starts
        for y in range(Y_SIZE)
    ]
    for copy in part_copies + pr_copies:
        copy.start()
    parts_ref[pl.ds(yd - yy, Y_SIZE)] = jnp.zeros((Y_SIZE, 4, LANES), jnp.float32)

    other_coef = zc_ref.at[pl.ds(0, len(zc_copies)), pl.ds(0, 6)]
    pltpu.make_async_copy(other_coef, other_coef, zc_recv).wait()

    def z_rows(ref, half, k):
        flat = ref.reshape(ref.shape[0] * 8, LANES)
        return jnp.stack(
            [
                jnp.stack([flat[pl.ds(half * h + 2 * k + t, Z_SIZE, stride=8), :] for t in range(2)])
                for h in range(2)
            ]
        )

    z_coef, z_saved = sub_coef([z_rows(zc_ref, 8 * Z_SIZE, k) for k in range(3)], steps)
    z_ring = ring_coef([value[0] for value in z_coef], [value[1] for value in z_coef])

    for copy in pr_copies:
        copy.wait_recv()
    p_side, p_mid = sub_side([group_rows(pr_ref, k) for k in range(2)], p_saved, p_steps)

    others = parts_ref.at[pl.ds(0, len(part_copies))]
    pltpu.make_async_copy(others, others, part_recv).wait()
    for h in range(2):
        for z in range(Z_SIZE):
            first = h * (Z_SIZE * Y_SIZE) + z * Y_SIZE
            total = parts_ref[first] + parts_ref[first + 1] + (parts_ref[first + 2] + parts_ref[first + 3])
            sums_ref[z, 4 * h : 4 * h + 4, :] = total
    for k in range(2):
        for t in range(2):
            sums_ref[zz, pl.ds(4 * xlo + 2 * k + t, 1), :] = p_side[k][t, 0:1]
    z_side, z_mid = sub_side([z_rows(sums_ref, 4, k) for k in range(2)], z_saved, steps)
    u_p, u_q = ring_solve(z_ring, [value[0] for value in z_side], [value[1] for value in z_side])

    lower = xlo == 0
    u_p, u_q = spread(u_p), spread(u_q)
    u_left, u_right = jnp.where(lower, u_p, u_q), jnp.where(lower, u_q, u_p)
    own_saved = [tuple(jnp.where(lower, value[0], value[1]) for value in factors) for factors in z_saved]
    own_mid = [jnp.where(lower, value[0], value[1]) for value in z_mid]
    u_left, u_right = sub_back(own_saved, own_mid, steps, u_left, u_right)
    u_left, u_right = at_row(u_left, zz), at_row(u_right, zz)
    u_left, u_right = sub_back(p_saved, p_mid, p_steps, u_left, u_right)
    u_left, u_right = at_row(u_left, yy), at_row(u_right, yy)
    u_left, u_right = sub_back(ys_saved, ys_mid, steps, u_left, u_right)
    updated = chain_back(y_saved, y_mid, u_left, u_right)
    for v in range(8):
        for t in range(2):
            out_ref[pl.ds(2 * v + t, SUB, stride=16), :] = updated[v, t]

    for copy in x_copies + pc_copies + pr_copies:
        copy.wait_send()
    pltpu.make_async_copy(other_coef, other_coef, zc_send).wait()
    pltpu.make_async_copy(others, others, part_send).wait()


def local(mobile, dispersion_x, dispersion_y, capacity, immobile, exchange_rates, rate_shares):
    flat = [value.reshape(ROWS, LANES) for value in (mobile, dispersion_x, dispersion_y, capacity)]
    any_spec = pl.BlockSpec(memory_space=pl.ANY)
    square = pltpu.VMEM((ROWS, LANES), jnp.float32)
    zones = pltpu.SMEM((4,), jnp.float32)
    dma = pltpu.SemaphoreType.DMA
    updated = pl.pallas_call(
        kernel,
        out_shape=pltpu.VMEM((ROWS, LANES), jnp.float32),
        in_specs=[any_spec] * 7,
        out_specs=pl.BlockSpec(memory_space=pltpu.VMEM),
        scratch_shapes=[
            square, square, square, square, pltpu.VMEM((4 * ROWS, LANES), jnp.float32), zones, zones,
            square, square, square,
            pltpu.VMEM((XG_SIZE, 8, LANES), jnp.float32),
            pltpu.VMEM((SUB, 8, LANES), jnp.float32),
            pltpu.VMEM((SUB, 8, LANES), jnp.float32),
            pltpu.VMEM((XLO_SIZE * Z_SIZE, 8, LANES), jnp.float32),
            pltpu.VMEM((4, LANES), jnp.float32),
            pltpu.VMEM((PLANE * Z_SIZE, 4, LANES), jnp.float32),
            pltpu.VMEM((Z_SIZE, 8, LANES), jnp.float32),
            pltpu.VMEM((2, SUB, LANES), jnp.float32),
            dma((7,)),
            dma((XG_SIZE - 1,)), dma((XG_SIZE - 1,)),
            dma((Y_SIZE - 1,)), dma((Y_SIZE - 1,)), dma((Y_SIZE - 1,)), dma((Y_SIZE - 1,)),
            dma(()), dma(()), dma(()), dma(()),
            pltpu.SemaphoreType.REGULAR,
        ],
        compiler_params=pltpu.CompilerParams(collective_id=0, has_side_effects=True),
    )(*flat, immobile.reshape(4 * ROWS, LANES), exchange_rates, rate_shares)
    return updated.reshape(mobile.shape)


def solution(mesh):
    return jax.shard_map(
        local,
        mesh=mesh,
        in_specs=(
            P("yd", None, "xg"),
            P("yd", None, "xg"),
            P("yd", None, "xg"),
            P("yd", None, "xg"),
            P(None, "yd", None, "xg"),
            P(),
            P(),
        ),
        out_specs=P("yd", None, "xg"),
        check_vma=False,
    )
```

```python
import functools

import jax
import jax.numpy as jnp
from jax import lax
from jax.experimental import pallas as pl
from jax.experimental.pallas import tpu as pltpu
from jax.sharding import PartitionSpec as P

MESH = pl.DeviceIdType.MESH
Y_SIZE, Z_SIZE, XLO_SIZE, XG_SIZE = 4, 8, 2, 4
PLANE = XLO_SIZE * Y_SIZE
ROWS = 128
LANES = 128
SUB = 8

roll = pltpu.roll


def join_coef(left, right):
    e_a, gl_a, gr_a = left
    e_b, gl_b, gr_b = right
    ground = gr_a + gl_b
    inverse = 1.0 / (ground + (e_a + e_b))
    a = e_a * inverse
    b = e_b * inverse
    return (e_a * b, gl_a + a * ground, gr_b + b * ground), (a, b, inverse)


def join_side(left, right, factors):
    a, b, _ = factors
    middle = left[1] + right[0]
    return (left[0] + a * middle, right[1] + b * middle), middle


def between(factors, middle, u_left, u_right):
    a, b, inverse = factors
    carried = a * u_left + b * u_right
    return carried if middle is None else middle * inverse + carried


def halves(values):
    count = values.shape[0]
    pairs = values.reshape((count // 2, 2) + values.shape[1:])
    return pairs[:, 0], pairs[:, 1]


def woven(first, second):
    count = first.shape[0]
    return jnp.stack([first, second], axis=1).reshape((2 * count,) + first.shape[1:])


def chain_coef(face, ground):
    (e_a, e_b), (g_a, g_b) = halves(face), halves(ground)
    inverse = 1.0 / (g_a + (e_a + e_b))
    a = e_a * inverse
    b = e_b * inverse
    coef = (e_a * b, a * g_a, g_b + b * g_a)
    saved = [(a, b, inverse)]
    while coef[0].shape[0] > 1:
        split = [halves(value) for value in coef]
        coef, factors = join_coef([s[0] for s in split], [s[1] for s in split])
        saved.append(factors)
    return tuple(value[0] for value in coef), saved


def chain_side(source, saved):
    f_a, f_b = halves(source)
    a, b, _ = saved[0]
    side = (a * f_a, f_b + b * f_a)
    middles = [f_a]
    for factors in saved[1:]:
        split = [halves(value) for value in side]
        side, middle = join_side([s[0] for s in split], [s[1] for s in split], factors)
        middles.append(middle)
    return tuple(value[0] for value in side), middles


def chain_back(saved, middles, u_left, u_right):
    u_left, u_right = u_left[None], u_right[None]
    for level in reversed(range(len(saved))):
        u_mid = between(saved[level], middles[level], u_left, u_right)
        if level:
            u_left, u_right = woven(u_left, u_mid), woven(u_mid, u_right)
        else:
            u_right = woven(u_mid, u_right)
    return u_right


def ahead(value, steps):
    return roll(value, value.shape[-2] - steps, value.ndim - 2)


def behind(value, steps):
    return roll(value, steps, value.ndim - 2)


def sub_coef(coef, steps):
    saved = []
    for step in steps:
        coef, factors = join_coef(coef, [ahead(value, step) for value in coef])
        saved.append(factors)
    return coef, saved


def sub_side(side, saved, steps):
    middles = []
    for step, factors in zip(steps, saved):
        side, middle = join_side(side, [ahead(value, step) for value in side], factors)
        middles.append(middle)
    return side, middles


def sub_back(saved, middles, steps, u_left, u_right):
    place = lax.broadcasted_iota(jnp.int32, u_left.shape, u_left.ndim - 2)
    for step, factors, middle in reversed(list(zip(steps, saved, middles))):
        u_mid = between(factors, middle, u_left, u_right)
        first = (place & step) == 0
        u_left, u_right = (
            jnp.where(first, u_left, behind(u_mid, step)),
            jnp.where(first, u_mid, behind(u_right, step)),
        )
    return u_left, u_right


def ring_coef(first, second):
    link = first[0] + second[0]
    ground_q = first[2] + second[1]
    ground_p = second[2] + first[1]
    inverse = 1.0 / (ground_q * ground_p + link * (ground_q + ground_p))
    link = link * inverse
    return link, ground_p * inverse + link, ground_q * inverse + link


def ring_solve(ring, first, second):
    link, to_q, to_p = ring
    f_q = first[1] + second[0]
    f_p = second[1] + first[0]
    return to_p * f_p + link * f_q, to_q * f_q + link * f_p


def strided(ref, stride):
    return jnp.stack([ref[pl.ds(start, SUB, stride=stride), :] for start in range(stride)])


def kernel(
    mobile_hbm, dx_hbm, dy_hbm, cap_hbm, imm_hbm, rates_hbm, shares_hbm, out_ref,
    mobile_ref, dx_ref, dy_ref, cap_ref, imm_ref, rates_ref, shares_ref, sto_ref, work_ref, work2_ref,
    x_ref, pc_ref, pr_ref, zc_ref, part_ref, parts_ref, sums_ref, pick_ref, res_ref,
    in_sem, x_send, x_recv, pc_send, pc_recv, pr_send, pr_recv,
    zc_send, zc_recv, part_send, part_recv, ready,
):
    xg = lax.axis_index("xg")
    yd = lax.axis_index("yd")
    xlo = yd // (Z_SIZE * Y_SIZE)
    zz = (yd // Y_SIZE) % Z_SIZE
    yy = yd % Y_SIZE
    slot = xlo * Y_SIZE + yy

    loads = [
        pltpu.make_async_copy(src, dst, in_sem.at[i])
        for i, (src, dst) in enumerate(
            [
                (rates_hbm, rates_ref), (shares_hbm, shares_ref), (cap_hbm, cap_ref), (dy_hbm, dy_ref),
                (dx_hbm, dx_ref), (imm_hbm, imm_ref), (mobile_hbm, mobile_ref),
            ]
        )
    ]

    def turned(position, steps, size):
        return jnp.where(position >= size - steps, steps - size, steps)

    across = jnp.where(xlo == 0, Z_SIZE * Y_SIZE, -Z_SIZE * Y_SIZE)
    y_turns = [turned(yy, k, Y_SIZE) for k in range(1, Y_SIZE)]
    x_peers = [{"xg": xg + turned(xg, k, XG_SIZE), "yd": yd} for k in range(1, XG_SIZE)]
    y_peers = [{"xg": xg, "yd": yd + turn} for turn in y_turns]
    plane_peers = y_peers + [{"xg": xg, "yd": yd + across + turn} for turn in [0] + y_turns]
    z_turns = [turned(zz, k, Z_SIZE) * Y_SIZE for k in range(Z_SIZE)]
    z_twos = [{"xg": xg, "yd": yd + z_turns[k]} for k in (2, Z_SIZE - 2)]
    z_near = z_twos + [{"xg": xg, "yd": yd + z_turns[k]} for k in (1, Z_SIZE - 1)]
    entered = plane_peers[::-1] + x_peers + z_near
    barrier = pltpu.get_barrier_semaphore()

    @pl.when(yd >= 0)
    def _():
        for peer in entered:
            pl.semaphore_signal(barrier, inc=1, device_id=peer, device_id_type=MESH)

    for load in loads:
        load.start()

    firsts = [h * (Z_SIZE * Y_SIZE) + z * Y_SIZE for z in range(Z_SIZE) for h in range(XLO_SIZE)]
    column = zz * XLO_SIZE + xlo
    starts = [jnp.where(column <= k, firsts[k + 1], firsts[k]) for k in range(len(firsts) - 1)]

    pc_ref[Y_SIZE:] = jnp.ones((Y_SIZE, 8, LANES), jnp.float32)
    pr_ref[Y_SIZE:] = jnp.zeros((Y_SIZE, 8, LANES), jnp.float32)

    def sends(ref, position, peers, send_sem, recv_sem):
        part = ref.at[position]
        return [
            pltpu.make_async_remote_copy(
                src_ref=part, dst_ref=part, send_sem=send_sem.at[k], recv_sem=recv_sem.at[k],
                device_id=peer, device_id_type=MESH,
            )
            for k, peer in enumerate(peers)
        ]

    loads[0].wait()
    loads[1].wait()
    weights = []
    for k in range(4):
        rate = jnp.full((SUB, LANES), rates_ref[k], jnp.float32)
        weights.append(rate * jnp.full((SUB, LANES), shares_ref[k], jnp.float32) / (1.0 + rate))
    loads[2].wait()
    capacity = cap_ref[...].reshape(16, SUB, LANES)
    storage = 1.0 + capacity * (weights[0] + weights[1] + weights[2] + weights[3])
    storage = storage.reshape(ROWS, LANES)
    sto_ref[...] = storage

    steps = (1, 2, 4)
    loads[3].wait()
    y_face = strided(dy_ref, 16).reshape(8, 2, SUB, LANES)
    y_ground = strided(sto_ref, 16).reshape(8, 2, SUB, LANES)
    y_coef, y_saved = chain_coef(y_face, y_ground)
    y_coef, ys_saved = sub_coef(y_coef, steps)
    for k in range(3):
        for t in range(2):
            pc_ref[yy, pl.ds(2 * k + t, 1), :] = y_coef[k][t, 0:1]

    loads[4].wait()
    work_ref[...] = jnp.transpose(dx_ref[...])
    work2_ref[...] = jnp.transpose(storage)
    x_coef, x_saved = chain_coef(strided(work_ref, 16), strided(work2_ref, 16))
    loads[5].wait()
    loads[6].wait()
    imm = imm_ref[...].reshape(4, 16, SUB, LANES)
    mixed = weights[0] * imm[0] + weights[1] * imm[1] + weights[2] * imm[2] + weights[3] * imm[3]
    source = mobile_ref[...].reshape(16, SUB, LANES) + capacity * mixed
    work_ref[...] = jnp.transpose(source.reshape(ROWS, LANES))
    x_side, x_mid = chain_side(strided(work_ref, 16), x_saved)
    x_coef, xs_saved = sub_coef(x_coef, steps)
    x_side, xs_mid = sub_side(x_side, xs_saved, steps)

    def next_lane(value):
        return roll(value, LANES - 1, 1)

    even = (lax.broadcasted_iota(jnp.int32, (SUB, LANES), 1) & 1) == 0

    def both_lanes(value):
        value = jnp.where(even, value, roll(value, 1, 1))
        return jnp.broadcast_to(value[0:1], (SUB, LANES))

    own_coef, half_factors = join_coef(x_coef, [next_lane(value) for value in x_coef])
    own_side, half_middle = join_side(x_side, [next_lane(value) for value in x_side], half_factors)
    own_coef = [both_lanes(value) for value in own_coef]
    own_side = [both_lanes(value) for value in own_side]
    for k, value in enumerate(own_coef + own_side):
        x_ref[0, pl.ds(k, 1), :] = value[0:1]

    pl.semaphore_wait(barrier, len(entered))

    x_copies = [
        pltpu.make_async_remote_copy(
            src_ref=x_ref.at[0], dst_ref=x_ref.at[XG_SIZE - k], send_sem=x_send.at[k - 1],
            recv_sem=x_recv.at[k - 1], device_id=x_peers[k - 1], device_id_type=MESH,
        )
        for k in range(1, XG_SIZE)
    ]
    pc_copies = sends(pc_ref, yy, y_peers, pc_send, pc_recv)
    for copy in x_copies + pc_copies:
        copy.start()
    for peer in z_near:
        pl.semaphore_signal(ready.at[0], inc=1, device_id=peer, device_id_type=MESH)
    pl.semaphore_wait(ready.at[0], len(z_near))
    for peer in z_twos:
        pl.semaphore_signal(ready.at[1], inc=1, device_id=peer, device_id_type=MESH)

    one = jnp.ones((SUB, LANES), jnp.float32)
    none = jnp.zeros((SUB, LANES), jnp.float32)

    def responses(saved, subs, middles, sub_middles, u_left, u_right, out):
        u_left, u_right = sub_back(subs, sub_middles, steps, u_left, u_right)
        cells = chain_back(saved, middles, u_left, u_right).reshape(16, SUB, LANES)
        for v in range(16):
            out[pl.ds(v, SUB, stride=16), :] = cells[v]
        return out[...]

    no_mid = [None] * len(x_mid)
    no_sub = [None] * len(steps)
    still = responses(x_saved, xs_saved, x_mid, xs_mid, none, none, work_ref)
    by_left = responses(x_saved, xs_saved, no_mid, no_sub, one, none, work2_ref)
    by_right = responses(x_saved, xs_saved, no_mid, no_sub, none, one, res_ref.at[0])
    half_still = both_lanes(half_middle * half_factors[2])[0:1]
    half_before = both_lanes(half_factors[0])[0:1]
    half_last = both_lanes(half_factors[1])[0:1]
    first = even[0:1]
    res_ref[0] = still + jnp.where(first, by_right, by_left) * half_still
    res_ref[1] = jnp.where(first, by_left + by_right * half_before, by_left * half_before)
    res_ref[2] = jnp.where(first, by_right * half_last, by_right + by_left * half_last)

    both = jnp.ones((2, SUB, LANES), jnp.float32)
    neither = jnp.zeros((2, SUB, LANES), jnp.float32)
    no_mid = [None] * len(y_saved)
    res_ref[3] = responses(y_saved, ys_saved, no_mid, no_sub, both, neither, work_ref) * sto_ref[...]
    res_ref[4] = responses(y_saved, ys_saved, no_mid, no_sub, neither, both, work2_ref) * sto_ref[...]

    for copy in pc_copies:
        copy.wait_recv()

    def group_rows(ref, k):
        flat = ref.reshape(SUB * 8, LANES)
        return jnp.stack([flat[pl.ds(2 * k + t, SUB, stride=8), :] for t in range(2)])

    def spread(value):
        return jnp.broadcast_to(value[:, 0:1], value.shape)

    def at_row(value, place):
        for t in range(2):
            pick_ref[t] = value[t]
        return jnp.stack([pick_ref[t, pl.ds(place, SUB, stride=0), :] for t in range(2)])

    p_steps = (1, 2)
    p_coef, p_saved = sub_coef([group_rows(pc_ref, k) for k in range(3)], p_steps)
    own = xlo * Z_SIZE + zz
    for k in range(3):
        for t in range(2):
            zc_ref[own, pl.ds(2 * k + t, 1), :] = p_coef[k][t, 0:1]
    zc_part = zc_ref.at[own, pl.ds(0, 6)]
    zc_places = [yd - zz * Y_SIZE + jnp.where(zz <= k, k + 1, k) * Y_SIZE for k in range(Z_SIZE - 1)]
    zc_places += [yd + across + z_turns[k] for k in (0, 1, 7, 2, 6, 3, 5, 4)]
    zc_copies = [
        pltpu.make_async_remote_copy(
            src_ref=zc_part, dst_ref=zc_part, send_sem=zc_send, recv_sem=zc_recv,
            device_id={"xg": xg, "yd": place}, device_id_type=MESH,
        )
        for place in zc_places
    ]
    for copy in zc_copies[:-3]:
        copy.start()

    place = lax.broadcasted_iota(jnp.int32, (2, SUB, LANES), 1)
    unit = jnp.where(place == yy, 1.0, 0.0)
    zero = jnp.zeros_like(unit)
    from_left, _ = sub_side((unit, zero), p_saved, p_steps)
    from_right, _ = sub_side((zero, unit), p_saved, p_steps)
    row = lax.broadcasted_iota(jnp.int32, (SUB, LANES), 0)

    def in_rows(pair):
        (a, b), (c, d) = [spread(value) for value in pair]
        return jnp.where(row == 0, a, jnp.where(row == 1, b, jnp.where(row == 2, c, d)))

    from_left = in_rows(from_left)
    from_right = in_rows(from_right)

    for copy in x_copies:
        copy.wait_recv()

    def block(g):
        rows = [jnp.broadcast_to(x_ref[g, pl.ds(k, 1), :], (SUB, LANES)) for k in range(5)]
        return rows[:3], rows[3:]

    rest_coef, rest_side = block(1)
    for g in (2, 3):
        coef, side = block(g)
        rest_coef, factors = join_coef(rest_coef, coef)
        rest_side, _ = join_side(rest_side, side, factors)
    u_before, u_last = ring_solve(ring_coef(own_coef, rest_coef), own_side, rest_side)
    after_x = jnp.transpose(res_ref[0] + res_ref[1] * u_before[0:1] + res_ref[2] * u_last[0:1])

    def total(weights):
        terms = (weights * after_x).reshape(16, SUB, LANES)
        while terms.shape[0] > 1:
            low, high = halves(terms)
            terms = low + high
        terms = terms[0] + roll(terms[0], 4, 0)
        return terms + roll(terms, 2, 0)

    f_left, f_right = total(res_ref[3]), total(res_ref[4])
    part_ref[...] = (from_left * f_left + from_right * f_right)[0:4]
    pr_ref[yy] = jnp.where(row < 2, f_left, f_right)
    pr_copies = sends(pr_ref, yy, y_peers, pr_send, pr_recv)
    part_copies = [
        pltpu.make_async_remote_copy(
            src_ref=part_ref, dst_ref=parts_ref.at[yd], send_sem=part_send, recv_sem=part_recv,
            device_id={"xg": xg, "yd": starts[k] + y}, device_id_type=MESH,
        )
        for k, y in sorted(
            ((k, y) for k in range(len(starts)) for y in range(Y_SIZE)),
            key=lambda place: (place[0] // 2 >= 4, min(place[1], 2), place),
        )
    ]
    for copy in pr_copies:
        copy.start()
    pl.semaphore_wait(ready.at[1], len(z_twos))
    for copy in zc_copies[-3:] + part_copies:
        copy.start()
    parts_ref[pl.ds(yd - yy, Y_SIZE)] = jnp.zeros((Y_SIZE, 4, LANES), jnp.float32)

    work_ref[...] = after_x * sto_ref[...]
    y_side, y_mid = chain_side(strided(work_ref, 16).reshape(8, 2, SUB, LANES), y_saved)
    _, ys_mid = sub_side(y_side, ys_saved, steps)

    other_coef = zc_ref.at[pl.ds(0, len(zc_copies)), pl.ds(0, 6)]
    pltpu.make_async_copy(other_coef, other_coef, zc_recv).wait()

    def z_rows(ref, half, k):
        flat = ref.reshape(ref.shape[0] * 8, LANES)
        return jnp.stack(
            [
                jnp.stack([flat[pl.ds(half * h + 2 * k + t, Z_SIZE, stride=8), :] for t in range(2)])
                for h in range(2)
            ]
        )

    z_coef, z_saved = sub_coef([z_rows(zc_ref, 8 * Z_SIZE, k) for k in range(3)], steps)
    z_ring = ring_coef([value[0] for value in z_coef], [value[1] for value in z_coef])

    for copy in pr_copies:
        copy.wait_recv()
    p_side, p_mid = sub_side([group_rows(pr_ref, k) for k in range(2)], p_saved, p_steps)

    others = parts_ref.at[pl.ds(0, len(part_copies))]
    pltpu.make_async_copy(others, others, part_recv).wait()
    for h in range(2):
        for z in range(Z_SIZE):
            first = h * (Z_SIZE * Y_SIZE) + z * Y_SIZE
            total = parts_ref[first] + parts_ref[first + 1] + (parts_ref[first + 2] + parts_ref[first + 3])
            sums_ref[z, 4 * h : 4 * h + 4, :] = total
    for k in range(2):
        for t in range(2):
            sums_ref[zz, pl.ds(4 * xlo + 2 * k + t, 1), :] = p_side[k][t, 0:1]
    z_side, z_mid = sub_side([z_rows(sums_ref, 4, k) for k in range(2)], z_saved, steps)
    u_p, u_q = ring_solve(z_ring, [value[0] for value in z_side], [value[1] for value in z_side])

    lower = xlo == 0
    u_p, u_q = spread(u_p), spread(u_q)
    u_left, u_right = jnp.where(lower, u_p, u_q), jnp.where(lower, u_q, u_p)
    own_saved = [tuple(jnp.where(lower, value[0], value[1]) for value in factors) for factors in z_saved]
    own_mid = [jnp.where(lower, value[0], value[1]) for value in z_mid]
    u_left, u_right = sub_back(own_saved, own_mid, steps, u_left, u_right)
    u_left, u_right = at_row(u_left, zz), at_row(u_right, zz)
    u_left, u_right = sub_back(p_saved, p_mid, p_steps, u_left, u_right)
    u_left, u_right = at_row(u_left, yy), at_row(u_right, yy)
    u_left, u_right = sub_back(ys_saved, ys_mid, steps, u_left, u_right)
    updated = chain_back(y_saved, y_mid, u_left, u_right)
    for v in range(8):
        for t in range(2):
            out_ref[pl.ds(2 * v + t, SUB, stride=16), :] = updated[v, t]

    for copy in x_copies + pc_copies + pr_copies:
        copy.wait_send()
    pltpu.make_async_copy(other_coef, other_coef, zc_send).wait()
    pltpu.make_async_copy(others, others, part_send).wait()


def local(mobile, dispersion_x, dispersion_y, capacity, immobile, exchange_rates, rate_shares):
    flat = [value.reshape(ROWS, LANES) for value in (mobile, dispersion_x, dispersion_y, capacity)]
    any_spec = pl.BlockSpec(memory_space=pl.ANY)
    square = pltpu.VMEM((ROWS, LANES), jnp.float32)
    zones = pltpu.SMEM((4,), jnp.float32)
    dma = pltpu.SemaphoreType.DMA
    updated = pl.pallas_call(
        kernel,
        out_shape=pltpu.VMEM((ROWS, LANES), jnp.float32),
        in_specs=[any_spec] * 7,
        out_specs=pl.BlockSpec(memory_space=pltpu.VMEM),
        scratch_shapes=[
            square, square, square, square, pltpu.VMEM((4 * ROWS, LANES), jnp.float32), zones, zones,
            square, square, square,
            pltpu.VMEM((XG_SIZE, 8, LANES), jnp.float32),
            pltpu.VMEM((SUB, 8, LANES), jnp.float32),
            pltpu.VMEM((SUB, 8, LANES), jnp.float32),
            pltpu.VMEM((XLO_SIZE * Z_SIZE, 8, LANES), jnp.float32),
            pltpu.VMEM((4, LANES), jnp.float32),
            pltpu.VMEM((PLANE * Z_SIZE, 4, LANES), jnp.float32),
            pltpu.VMEM((Z_SIZE, 8, LANES), jnp.float32),
            pltpu.VMEM((2, SUB, LANES), jnp.float32),
            pltpu.VMEM((5, ROWS, LANES), jnp.float32),
            dma((7,)),
            dma((XG_SIZE - 1,)), dma((XG_SIZE - 1,)),
            dma((Y_SIZE - 1,)), dma((Y_SIZE - 1,)), dma((Y_SIZE - 1,)), dma((Y_SIZE - 1,)),
            dma(()), dma(()), dma(()), dma(()),
            pltpu.SemaphoreType.REGULAR((2,)),
        ],
        compiler_params=pltpu.CompilerParams(collective_id=0, has_side_effects=True),
    )(*flat, immobile.reshape(4 * ROWS, LANES), exchange_rates, rate_shares)
    return updated.reshape(mobile.shape)


def solution(mesh):
    return jax.shard_map(
        local,
        mesh=mesh,
        in_specs=(
            P("yd", None, "xg"),
            P("yd", None, "xg"),
            P("yd", None, "xg"),
            P("yd", None, "xg"),
            P(None, "yd", None, "xg"),
            P(),
            P(),
        ),
        out_specs=P("yd", None, "xg"),
        check_vma=False,
    )
```

```python
import functools

import jax
import jax.numpy as jnp
from jax import lax
from jax.experimental import pallas as pl
from jax.experimental.pallas import tpu as pltpu
from jax.sharding import PartitionSpec as P

MESH = pl.DeviceIdType.MESH
Y_SIZE, Z_SIZE, XLO_SIZE, XG_SIZE = 4, 8, 2, 4
PLANE = XLO_SIZE * Y_SIZE
ROWS = 128
LANES = 128
SUB = 8

roll = pltpu.roll


def join_coef(left, right):
    e_a, gl_a, gr_a = left
    e_b, gl_b, gr_b = right
    ground = gr_a + gl_b
    inverse = 1.0 / (ground + (e_a + e_b))
    a = e_a * inverse
    b = e_b * inverse
    return (e_a * b, gl_a + a * ground, gr_b + b * ground), (a, b, inverse)


def join_side(left, right, factors):
    a, b, _ = factors
    middle = left[1] + right[0]
    return (left[0] + a * middle, right[1] + b * middle), middle


def between(factors, middle, u_left, u_right):
    a, b, inverse = factors
    carried = a * u_left + b * u_right
    return carried if middle is None else middle * inverse + carried


def halves(values):
    count = values.shape[0]
    pairs = values.reshape((count // 2, 2) + values.shape[1:])
    return pairs[:, 0], pairs[:, 1]


def woven(first, second):
    count = first.shape[0]
    return jnp.stack([first, second], axis=1).reshape((2 * count,) + first.shape[1:])


def chain_coef(face, ground):
    (e_a, e_b), (g_a, g_b) = halves(face), halves(ground)
    inverse = 1.0 / (g_a + (e_a + e_b))
    a = e_a * inverse
    b = e_b * inverse
    coef = (e_a * b, a * g_a, g_b + b * g_a)
    saved = [(a, b, inverse)]
    while coef[0].shape[0] > 1:
        split = [halves(value) for value in coef]
        coef, factors = join_coef([s[0] for s in split], [s[1] for s in split])
        saved.append(factors)
    return tuple(value[0] for value in coef), saved


def chain_side(source, saved):
    f_a, f_b = halves(source)
    a, b, _ = saved[0]
    side = (a * f_a, f_b + b * f_a)
    middles = [f_a]
    for factors in saved[1:]:
        split = [halves(value) for value in side]
        side, middle = join_side([s[0] for s in split], [s[1] for s in split], factors)
        middles.append(middle)
    return tuple(value[0] for value in side), middles


def chain_back(saved, middles, u_left, u_right):
    u_left, u_right = u_left[None], u_right[None]
    for level in reversed(range(len(saved))):
        u_mid = between(saved[level], middles[level], u_left, u_right)
        if level:
            u_left, u_right = woven(u_left, u_mid), woven(u_mid, u_right)
        else:
            u_right = woven(u_mid, u_right)
    return u_right


def ahead(value, steps):
    return roll(value, value.shape[-2] - steps, value.ndim - 2)


def behind(value, steps):
    return roll(value, steps, value.ndim - 2)


def sub_coef(coef, steps):
    saved = []
    for step in steps:
        coef, factors = join_coef(coef, [ahead(value, step) for value in coef])
        saved.append(factors)
    return coef, saved


def sub_side(side, saved, steps):
    middles = []
    for step, factors in zip(steps, saved):
        side, middle = join_side(side, [ahead(value, step) for value in side], factors)
        middles.append(middle)
    return side, middles


def sub_back(saved, middles, steps, u_left, u_right):
    place = lax.broadcasted_iota(jnp.int32, u_left.shape, u_left.ndim - 2)
    for step, factors, middle in reversed(list(zip(steps, saved, middles))):
        u_mid = between(factors, middle, u_left, u_right)
        first = (place & step) == 0
        u_left, u_right = (
            jnp.where(first, u_left, behind(u_mid, step)),
            jnp.where(first, u_mid, behind(u_right, step)),
        )
    return u_left, u_right


def ring_coef(first, second):
    link = first[0] + second[0]
    ground_q = first[2] + second[1]
    ground_p = second[2] + first[1]
    inverse = 1.0 / (ground_q * ground_p + link * (ground_q + ground_p))
    link = link * inverse
    return link, ground_p * inverse + link, ground_q * inverse + link


def ring_solve(ring, first, second):
    link, to_q, to_p = ring
    f_q = first[1] + second[0]
    f_p = second[1] + first[0]
    return to_p * f_p + link * f_q, to_q * f_q + link * f_p


def strided(ref, stride):
    return jnp.stack([ref[pl.ds(start, SUB, stride=stride), :] for start in range(stride)])


def kernel(
    mobile_hbm, dx_hbm, dy_hbm, cap_hbm, imm_hbm, rates_hbm, shares_hbm, out_ref,
    mobile_ref, dx_ref, dy_ref, cap_ref, imm_ref, rates_ref, shares_ref, sto_ref, work_ref, work2_ref,
    x_ref, pc_ref, pr_ref, zc_ref, part_ref, parts_ref, sums_ref, pick_ref, res_ref,
    in_sem, x_send, x_recv, pc_send, pc_recv, pr_send, pr_recv,
    zc_send, zc_recv, part_send, part_recv, ready,
):
    xg = lax.axis_index("xg")
    yd = lax.axis_index("yd")
    xlo = yd // (Z_SIZE * Y_SIZE)
    zz = (yd // Y_SIZE) % Z_SIZE
    yy = yd % Y_SIZE
    slot = xlo * Y_SIZE + yy

    loads = [
        pltpu.make_async_copy(src, dst, in_sem.at[i])
        for i, (src, dst) in enumerate(
            [
                (rates_hbm, rates_ref), (shares_hbm, shares_ref), (cap_hbm, cap_ref), (dy_hbm, dy_ref),
                (dx_hbm, dx_ref), (imm_hbm, imm_ref), (mobile_hbm, mobile_ref),
            ]
        )
    ]

    def turned(position, steps, size):
        return jnp.where(position >= size - steps, steps - size, steps)

    across = jnp.where(xlo == 0, Z_SIZE * Y_SIZE, -Z_SIZE * Y_SIZE)
    y_turns = [turned(yy, k, Y_SIZE) for k in range(1, Y_SIZE)]
    x_peers = [{"xg": xg + turned(xg, k, XG_SIZE), "yd": yd} for k in range(1, XG_SIZE)]
    y_peers = [{"xg": xg, "yd": yd + turn} for turn in y_turns]
    plane_peers = y_peers + [{"xg": xg, "yd": yd + across + turn} for turn in [0] + y_turns]
    z_turns = [turned(zz, k, Z_SIZE) * Y_SIZE for k in range(Z_SIZE)]
    z_twos = [{"xg": xg, "yd": yd + z_turns[k]} for k in (2, Z_SIZE - 2)]
    z_near = z_twos + [{"xg": xg, "yd": yd + z_turns[k]} for k in (1, Z_SIZE - 1)]
    entered = plane_peers[::-1] + x_peers + z_near
    barrier = pltpu.get_barrier_semaphore()

    @pl.when(yd >= 0)
    def _():
        for peer in entered:
            pl.semaphore_signal(barrier, inc=1, device_id=peer, device_id_type=MESH)

    for load in loads:
        load.start()

    firsts = [h * (Z_SIZE * Y_SIZE) + z * Y_SIZE for z in range(Z_SIZE) for h in range(XLO_SIZE)]
    column = zz * XLO_SIZE + xlo
    starts = [jnp.where(column <= k, firsts[k + 1], firsts[k]) for k in range(len(firsts) - 1)]

    pc_ref[Y_SIZE:] = jnp.ones((Y_SIZE, 8, LANES), jnp.float32)
    pr_ref[Y_SIZE:] = jnp.zeros((Y_SIZE, 8, LANES), jnp.float32)

    def sends(ref, position, peers, send_sem, recv_sem):
        part = ref.at[position]
        return [
            pltpu.make_async_remote_copy(
                src_ref=part, dst_ref=part, send_sem=send_sem.at[k], recv_sem=recv_sem.at[k],
                device_id=peer, device_id_type=MESH,
            )
            for k, peer in enumerate(peers)
        ]

    loads[0].wait()
    loads[1].wait()
    weights = []
    for k in range(4):
        rate = jnp.full((SUB, LANES), rates_ref[k], jnp.float32)
        weights.append(rate * jnp.full((SUB, LANES), shares_ref[k], jnp.float32) / (1.0 + rate))
    loads[2].wait()
    capacity = cap_ref[...].reshape(16, SUB, LANES)
    storage = 1.0 + capacity * (weights[0] + weights[1] + weights[2] + weights[3])
    storage = storage.reshape(ROWS, LANES)
    sto_ref[...] = storage

    steps = (1, 2, 4)
    loads[3].wait()
    y_face = strided(dy_ref, 16).reshape(8, 2, SUB, LANES)
    y_ground = strided(sto_ref, 16).reshape(8, 2, SUB, LANES)
    y_coef, y_saved = chain_coef(y_face, y_ground)
    y_coef, ys_saved = sub_coef(y_coef, steps)
    for k in range(3):
        for t in range(2):
            pc_ref[yy, pl.ds(2 * k + t, 1), :] = y_coef[k][t, 0:1]

    loads[4].wait()
    work_ref[...] = jnp.transpose(dx_ref[...])
    work2_ref[...] = jnp.transpose(storage)
    x_coef, x_saved = chain_coef(strided(work_ref, 16), strided(work2_ref, 16))
    loads[5].wait()
    loads[6].wait()
    imm = imm_ref[...].reshape(4, 16, SUB, LANES)
    mixed = weights[0] * imm[0] + weights[1] * imm[1] + weights[2] * imm[2] + weights[3] * imm[3]
    source = mobile_ref[...].reshape(16, SUB, LANES) + capacity * mixed
    work_ref[...] = jnp.transpose(source.reshape(ROWS, LANES))
    x_side, x_mid = chain_side(strided(work_ref, 16), x_saved)
    x_coef, xs_saved = sub_coef(x_coef, steps)
    x_side, xs_mid = sub_side(x_side, xs_saved, steps)

    def next_lane(value):
        return roll(value, LANES - 1, 1)

    even = (lax.broadcasted_iota(jnp.int32, (SUB, LANES), 1) & 1) == 0

    def both_lanes(value):
        value = jnp.where(even, value, roll(value, 1, 1))
        return jnp.broadcast_to(value[0:1], (SUB, LANES))

    own_coef, half_factors = join_coef(x_coef, [next_lane(value) for value in x_coef])
    own_side, half_middle = join_side(x_side, [next_lane(value) for value in x_side], half_factors)
    own_coef = [both_lanes(value) for value in own_coef]
    own_side = [both_lanes(value) for value in own_side]
    for k, value in enumerate(own_coef + own_side):
        x_ref[0, pl.ds(k, 1), :] = value[0:1]

    pl.semaphore_wait(barrier, len(entered))

    x_copies = [
        pltpu.make_async_remote_copy(
            src_ref=x_ref.at[0], dst_ref=x_ref.at[XG_SIZE - k], send_sem=x_send.at[k - 1],
            recv_sem=x_recv.at[k - 1], device_id=x_peers[k - 1], device_id_type=MESH,
        )
        for k in range(1, XG_SIZE)
    ]
    pc_copies = sends(pc_ref, yy, y_peers, pc_send, pc_recv)
    for copy in x_copies + pc_copies:
        copy.start()
    for peer in z_near:
        pl.semaphore_signal(ready.at[0], inc=1, device_id=peer, device_id_type=MESH)
    pl.semaphore_wait(ready.at[0], len(z_near))
    for peer in z_twos:
        pl.semaphore_signal(ready.at[1], inc=1, device_id=peer, device_id_type=MESH)

    one = jnp.ones((SUB, LANES), jnp.float32)
    none = jnp.zeros((SUB, LANES), jnp.float32)

    def responses(saved, subs, middles, sub_middles, u_left, u_right, out):
        u_left, u_right = sub_back(subs, sub_middles, steps, u_left, u_right)
        cells = chain_back(saved, middles, u_left, u_right).reshape(16, SUB, LANES)
        for v in range(16):
            out[pl.ds(v, SUB, stride=16), :] = cells[v]
        return out[...]

    no_mid = [None] * len(x_mid)
    no_sub = [None] * len(steps)
    still = responses(x_saved, xs_saved, x_mid, xs_mid, none, none, work_ref)
    by_left = responses(x_saved, xs_saved, no_mid, no_sub, one, none, work2_ref)
    by_right = responses(x_saved, xs_saved, no_mid, no_sub, none, one, res_ref.at[0])
    half_still = both_lanes(half_middle * half_factors[2])[0:1]
    half_before = both_lanes(half_factors[0])[0:1]
    half_last = both_lanes(half_factors[1])[0:1]
    first = even[0:1]
    res_ref[0] = still + jnp.where(first, by_right, by_left) * half_still
    res_ref[1] = jnp.where(first, by_left + by_right * half_before, by_left * half_before)
    res_ref[2] = jnp.where(first, by_right * half_last, by_right + by_left * half_last)

    both = jnp.ones((2, SUB, LANES), jnp.float32)
    neither = jnp.zeros((2, SUB, LANES), jnp.float32)
    no_mid = [None] * len(y_saved)
    res_ref[5] = responses(y_saved, ys_saved, no_mid, no_sub, both, neither, work_ref)
    res_ref[6] = responses(y_saved, ys_saved, no_mid, no_sub, neither, both, work2_ref)
    res_ref[3] = res_ref[5] * sto_ref[...]
    res_ref[4] = res_ref[6] * sto_ref[...]

    for copy in pc_copies:
        copy.wait_recv()

    def group_rows(ref, k):
        flat = ref.reshape(SUB * 8, LANES)
        return jnp.stack([flat[pl.ds(2 * k + t, SUB, stride=8), :] for t in range(2)])

    def spread(value):
        return jnp.broadcast_to(value[:, 0:1], value.shape)

    def at_row(value, place):
        for t in range(2):
            pick_ref[t] = value[t]
        return jnp.stack([pick_ref[t, pl.ds(place, SUB, stride=0), :] for t in range(2)])

    p_steps = (1, 2)
    p_coef, p_saved = sub_coef([group_rows(pc_ref, k) for k in range(3)], p_steps)
    own = xlo * Z_SIZE + zz
    for k in range(3):
        for t in range(2):
            zc_ref[own, pl.ds(2 * k + t, 1), :] = p_coef[k][t, 0:1]
    zc_part = zc_ref.at[own, pl.ds(0, 6)]
    zc_places = [yd - zz * Y_SIZE + jnp.where(zz <= k, k + 1, k) * Y_SIZE for k in range(Z_SIZE - 1)]
    zc_places += [yd + across + z_turns[k] for k in (0, 1, 7, 2, 6, 3, 5, 4)]
    zc_copies = [
        pltpu.make_async_remote_copy(
            src_ref=zc_part, dst_ref=zc_part, send_sem=zc_send, recv_sem=zc_recv,
            device_id={"xg": xg, "yd": place}, device_id_type=MESH,
        )
        for place in zc_places
    ]
    for copy in zc_copies[:4] + zc_copies[7:-3]:
        copy.start()

    place = lax.broadcasted_iota(jnp.int32, (2, SUB, LANES), 1)
    unit = jnp.where(place == yy, 1.0, 0.0)
    zero = jnp.zeros_like(unit)
    from_left, _ = sub_side((unit, zero), p_saved, p_steps)
    from_right, _ = sub_side((zero, unit), p_saved, p_steps)
    row = lax.broadcasted_iota(jnp.int32, (SUB, LANES), 0)

    def in_rows(pair):
        (a, b), (c, d) = [spread(value) for value in pair]
        return jnp.where(row == 0, a, jnp.where(row == 1, b, jnp.where(row == 2, c, d)))

    from_left = in_rows(from_left)
    from_right = in_rows(from_right)

    for copy in x_copies:
        copy.wait_recv()

    def block(g):
        rows = [jnp.broadcast_to(x_ref[g, pl.ds(k, 1), :], (SUB, LANES)) for k in range(5)]
        return rows[:3], rows[3:]

    rest_coef, rest_side = block(1)
    for g in (2, 3):
        coef, side = block(g)
        rest_coef, factors = join_coef(rest_coef, coef)
        rest_side, _ = join_side(rest_side, side, factors)
    u_before, u_last = ring_solve(ring_coef(own_coef, rest_coef), own_side, rest_side)
    after_x = jnp.transpose(res_ref[0] + res_ref[1] * u_before[0:1] + res_ref[2] * u_last[0:1])

    def total(weights):
        terms = (weights * after_x).reshape(16, SUB, LANES)
        while terms.shape[0] > 1:
            low, high = halves(terms)
            terms = low + high
        terms = terms[0] + roll(terms[0], 4, 0)
        return terms + roll(terms, 2, 0)

    f_left, f_right = total(res_ref[3]), total(res_ref[4])
    part_ref[...] = (from_left * f_left + from_right * f_right)[0:4]
    pr_ref[yy] = jnp.where(row < 2, f_left, f_right)
    pr_copies = sends(pr_ref, yy, y_peers, pr_send, pr_recv)
    part_copies = [
        pltpu.make_async_remote_copy(
            src_ref=part_ref, dst_ref=parts_ref.at[yd], send_sem=part_send, recv_sem=part_recv,
            device_id={"xg": xg, "yd": starts[k] + y}, device_id_type=MESH,
        )
        for k, y in sorted(
            ((k, y) for k in range(len(starts)) for y in range(Y_SIZE)),
            key=lambda place: (place[0] // 2 >= 4, min(place[1], 2), place),
        )
    ]
    for copy in pr_copies:
        copy.start()
    pl.semaphore_wait(ready.at[1], len(z_twos))
    for copy in zc_copies[-3:] + part_copies[:32] + zc_copies[4:7]:
        copy.start()
    parts_ref[pl.ds(yd - yy, Y_SIZE)] = jnp.zeros((Y_SIZE, 4, LANES), jnp.float32)

    work_ref[...] = after_x * sto_ref[...]
    y_side, y_mid = chain_side(strided(work_ref, 16).reshape(8, 2, SUB, LANES), y_saved)
    _, ys_mid = sub_side(y_side, ys_saved, steps)
    res_ref[7] = responses(y_saved, ys_saved, y_mid, ys_mid, neither, neither, work2_ref)

    def z_rows(ref, half, k):
        flat = ref.reshape(ref.shape[0] * 8, LANES)
        return jnp.stack(
            [
                jnp.stack([flat[pl.ds(half * h + 2 * k + t, Z_SIZE, stride=8), :] for t in range(2)])
                for h in range(2)
            ]
        )

    for copy in pr_copies:
        copy.wait_recv()
    for copy in part_copies[32:]:
        copy.start()
    p_side, p_mid = sub_side([group_rows(pr_ref, k) for k in range(2)], p_saved, p_steps)
    other_coef = zc_ref.at[pl.ds(0, len(zc_copies)), pl.ds(0, 6)]
    pltpu.make_async_copy(other_coef, other_coef, zc_recv).wait()

    z_coef, z_saved = sub_coef([z_rows(zc_ref, 8 * Z_SIZE, k) for k in range(3)], steps)
    z_ring = ring_coef([value[0] for value in z_coef], [value[1] for value in z_coef])


    others = parts_ref.at[pl.ds(0, len(part_copies))]
    pltpu.make_async_copy(others, others, part_recv).wait()
    for h in range(2):
        for z in range(Z_SIZE):
            first = h * (Z_SIZE * Y_SIZE) + z * Y_SIZE
            total = parts_ref[first] + parts_ref[first + 1] + (parts_ref[first + 2] + parts_ref[first + 3])
            sums_ref[z, 4 * h : 4 * h + 4, :] = total
    for k in range(2):
        for t in range(2):
            sums_ref[zz, pl.ds(4 * xlo + 2 * k + t, 1), :] = p_side[k][t, 0:1]
    z_side, z_mid = sub_side([z_rows(sums_ref, 4, k) for k in range(2)], z_saved, steps)
    u_p, u_q = ring_solve(z_ring, [value[0] for value in z_side], [value[1] for value in z_side])

    lower = xlo == 0
    u_p, u_q = spread(u_p), spread(u_q)
    u_left, u_right = jnp.where(lower, u_p, u_q), jnp.where(lower, u_q, u_p)
    own_saved = [tuple(jnp.where(lower, value[0], value[1]) for value in factors) for factors in z_saved]
    own_mid = [jnp.where(lower, value[0], value[1]) for value in z_mid]
    u_left, u_right = sub_back(own_saved, own_mid, steps, u_left, u_right)
    u_left, u_right = at_row(u_left, zz), at_row(u_right, zz)
    u_left, u_right = sub_back(p_saved, p_mid, p_steps, u_left, u_right)
    u_left, u_right = at_row(u_left, yy), at_row(u_right, yy)
    lower_half = (row & 1) == 0
    u_left = jnp.where(lower_half, u_left[0], u_left[1])
    u_right = jnp.where(lower_half, u_right[0], u_right[1])
    own, by_left, by_right = [res_ref[k].reshape(16, SUB, LANES) for k in (7, 5, 6)]
    out_ref[...] = (own + by_left * u_left + by_right * u_right).reshape(ROWS, LANES)

    for copy in x_copies + pc_copies + pr_copies:
        copy.wait_send()
    pltpu.make_async_copy(other_coef, other_coef, zc_send).wait()
    pltpu.make_async_copy(others, others, part_send).wait()


def local(mobile, dispersion_x, dispersion_y, capacity, immobile, exchange_rates, rate_shares):
    flat = [value.reshape(ROWS, LANES) for value in (mobile, dispersion_x, dispersion_y, capacity)]
    any_spec = pl.BlockSpec(memory_space=pl.ANY)
    square = pltpu.VMEM((ROWS, LANES), jnp.float32)
    zones = pltpu.SMEM((4,), jnp.float32)
    dma = pltpu.SemaphoreType.DMA
    updated = pl.pallas_call(
        kernel,
        out_shape=pltpu.VMEM((ROWS, LANES), jnp.float32),
        in_specs=[any_spec] * 7,
        out_specs=pl.BlockSpec(memory_space=pltpu.VMEM),
        scratch_shapes=[
            square, square, square, square, pltpu.VMEM((4 * ROWS, LANES), jnp.float32), zones, zones,
            square, square, square,
            pltpu.VMEM((XG_SIZE, 8, LANES), jnp.float32),
            pltpu.VMEM((SUB, 8, LANES), jnp.float32),
            pltpu.VMEM((SUB, 8, LANES), jnp.float32),
            pltpu.VMEM((XLO_SIZE * Z_SIZE, 8, LANES), jnp.float32),
            pltpu.VMEM((4, LANES), jnp.float32),
            pltpu.VMEM((PLANE * Z_SIZE, 4, LANES), jnp.float32),
            pltpu.VMEM((Z_SIZE, 8, LANES), jnp.float32),
            pltpu.VMEM((2, SUB, LANES), jnp.float32),
            pltpu.VMEM((8, ROWS, LANES), jnp.float32),
            dma((7,)),
            dma((XG_SIZE - 1,)), dma((XG_SIZE - 1,)),
            dma((Y_SIZE - 1,)), dma((Y_SIZE - 1,)), dma((Y_SIZE - 1,)), dma((Y_SIZE - 1,)),
            dma(()), dma(()), dma(()), dma(()),
            pltpu.SemaphoreType.REGULAR((2,)),
        ],
        compiler_params=pltpu.CompilerParams(collective_id=0, has_side_effects=True),
    )(*flat, immobile.reshape(4 * ROWS, LANES), exchange_rates, rate_shares)
    return updated.reshape(mobile.shape)


def solution(mesh):
    return jax.shard_map(
        local,
        mesh=mesh,
        in_specs=(
            P("yd", None, "xg"),
            P("yd", None, "xg"),
            P("yd", None, "xg"),
            P("yd", None, "xg"),
            P(None, "yd", None, "xg"),
            P(),
            P(),
        ),
        out_specs=P("yd", None, "xg"),
        check_vma=False,
    )
```

```python
import functools

import jax
import jax.numpy as jnp
from jax import lax
from jax.experimental import pallas as pl
from jax.experimental.pallas import tpu as pltpu
from jax.sharding import PartitionSpec as P

MESH = pl.DeviceIdType.MESH
Y_SIZE, Z_SIZE, XLO_SIZE, XG_SIZE = 4, 8, 2, 4
PLANE = XLO_SIZE * Y_SIZE
ROWS = 128
LANES = 128
SUB = 8

roll = pltpu.roll


def join_coef(left, right):
    e_a, gl_a, gr_a = left
    e_b, gl_b, gr_b = right
    ground = gr_a + gl_b
    inverse = 1.0 / (ground + (e_a + e_b))
    a = e_a * inverse
    b = e_b * inverse
    return (e_a * b, gl_a + a * ground, gr_b + b * ground), (a, b, inverse)


def join_side(left, right, factors):
    a, b, _ = factors
    middle = left[1] + right[0]
    return (left[0] + a * middle, right[1] + b * middle), middle


def between(factors, middle, u_left, u_right):
    a, b, inverse = factors
    carried = a * u_left + b * u_right
    return carried if middle is None else middle * inverse + carried


def halves(values):
    count = values.shape[0]
    pairs = values.reshape((count // 2, 2) + values.shape[1:])
    return pairs[:, 0], pairs[:, 1]


def woven(first, second):
    count = first.shape[0]
    return jnp.stack([first, second], axis=1).reshape((2 * count,) + first.shape[1:])


def chain_coef(face, ground):
    (e_a, e_b), (g_a, g_b) = halves(face), halves(ground)
    inverse = 1.0 / (g_a + (e_a + e_b))
    a = e_a * inverse
    b = e_b * inverse
    coef = (e_a * b, a * g_a, g_b + b * g_a)
    saved = [(a, b, inverse)]
    while coef[0].shape[0] > 1:
        split = [halves(value) for value in coef]
        coef, factors = join_coef([s[0] for s in split], [s[1] for s in split])
        saved.append(factors)
    return tuple(value[0] for value in coef), saved


def chain_side(source, saved):
    f_a, f_b = halves(source)
    a, b, _ = saved[0]
    side = (a * f_a, f_b + b * f_a)
    middles = [f_a]
    for factors in saved[1:]:
        split = [halves(value) for value in side]
        side, middle = join_side([s[0] for s in split], [s[1] for s in split], factors)
        middles.append(middle)
    return tuple(value[0] for value in side), middles


def chain_back(saved, middles, u_left, u_right):
    u_left, u_right = u_left[None], u_right[None]
    for level in reversed(range(len(saved))):
        u_mid = between(saved[level], middles[level], u_left, u_right)
        if level:
            u_left, u_right = woven(u_left, u_mid), woven(u_mid, u_right)
        else:
            u_right = woven(u_mid, u_right)
    return u_right


def ahead(value, steps):
    return roll(value, value.shape[-2] - steps, value.ndim - 2)


def behind(value, steps):
    return roll(value, steps, value.ndim - 2)


def sub_coef(coef, steps):
    saved = []
    for step in steps:
        coef, factors = join_coef(coef, [ahead(value, step) for value in coef])
        saved.append(factors)
    return coef, saved


def sub_side(side, saved, steps):
    middles = []
    for step, factors in zip(steps, saved):
        side, middle = join_side(side, [ahead(value, step) for value in side], factors)
        middles.append(middle)
    return side, middles


def sub_back(saved, middles, steps, u_left, u_right):
    place = lax.broadcasted_iota(jnp.int32, u_left.shape, u_left.ndim - 2)
    for step, factors, middle in reversed(list(zip(steps, saved, middles))):
        u_mid = between(factors, middle, u_left, u_right)
        first = (place & step) == 0
        u_left, u_right = (
            jnp.where(first, u_left, behind(u_mid, step)),
            jnp.where(first, u_mid, behind(u_right, step)),
        )
    return u_left, u_right


def ring_coef(first, second):
    link = first[0] + second[0]
    ground_q = first[2] + second[1]
    ground_p = second[2] + first[1]
    inverse = 1.0 / (ground_q * ground_p + link * (ground_q + ground_p))
    link = link * inverse
    return link, ground_p * inverse + link, ground_q * inverse + link


def ring_solve(ring, first, second):
    link, to_q, to_p = ring
    f_q = first[1] + second[0]
    f_p = second[1] + first[0]
    return to_p * f_p + link * f_q, to_q * f_q + link * f_p


def strided(ref, stride):
    return jnp.stack([ref[pl.ds(start, SUB, stride=stride), :] for start in range(stride)])


def kernel(
    mobile_hbm, dx_hbm, dy_hbm, cap_hbm, imm_hbm, rates_hbm, shares_hbm, out_ref,
    mobile_ref, dx_ref, dy_ref, cap_ref, imm_ref, rates_ref, shares_ref, sto_ref, work_ref, work2_ref,
    x_ref, pc_ref, pr_ref, zc_ref, part_ref, parts_ref, sums_ref, pick_ref, res_ref,
    in_sem, x_send, x_recv, pc_send, pc_recv, pr_send, pr_recv,
    zc_send, zc_recv, part_send, part_recv, ready,
):
    xg = lax.axis_index("xg")
    yd = lax.axis_index("yd")
    xlo = yd // (Z_SIZE * Y_SIZE)
    zz = (yd // Y_SIZE) % Z_SIZE
    yy = yd % Y_SIZE
    slot = xlo * Y_SIZE + yy

    loads = [
        pltpu.make_async_copy(src, dst, in_sem.at[i])
        for i, (src, dst) in enumerate(
            [
                (rates_hbm, rates_ref), (shares_hbm, shares_ref), (cap_hbm, cap_ref), (dy_hbm, dy_ref),
                (dx_hbm, dx_ref), (imm_hbm, imm_ref), (mobile_hbm, mobile_ref),
            ]
        )
    ]

    def turned(position, steps, size):
        return jnp.where(position >= size - steps, steps - size, steps)

    across = jnp.where(xlo == 0, Z_SIZE * Y_SIZE, -Z_SIZE * Y_SIZE)
    y_turns = [turned(yy, k, Y_SIZE) for k in range(1, Y_SIZE)]
    x_peers = [{"xg": xg + turned(xg, k, XG_SIZE), "yd": yd} for k in range(1, XG_SIZE)]
    y_peers = [{"xg": xg, "yd": yd + turn} for turn in y_turns]
    plane_peers = y_peers + [{"xg": xg, "yd": yd + across + turn} for turn in [0] + y_turns]
    z_turns = [turned(zz, k, Z_SIZE) * Y_SIZE for k in range(Z_SIZE)]
    z_twos = [{"xg": xg, "yd": yd + z_turns[k]} for k in (2, Z_SIZE - 2)]
    z_near = z_twos + [{"xg": xg, "yd": yd + z_turns[k]} for k in (1, Z_SIZE - 1)]
    entered = plane_peers[::-1] + x_peers + z_near
    barrier = pltpu.get_barrier_semaphore()

    @pl.when(yd >= 0)
    def _():
        for peer in entered:
            pl.semaphore_signal(barrier, inc=1, device_id=peer, device_id_type=MESH)

    for load in loads:
        load.start()

    firsts = [h * (Z_SIZE * Y_SIZE) + z * Y_SIZE for z in range(Z_SIZE) for h in range(XLO_SIZE)]
    column = zz * XLO_SIZE + xlo
    starts = [jnp.where(column <= k, firsts[k + 1], firsts[k]) for k in range(len(firsts) - 1)]

    pc_ref[Y_SIZE:] = jnp.ones((Y_SIZE, 8, LANES), jnp.float32)
    pr_ref[Y_SIZE:] = jnp.zeros((Y_SIZE, 8, LANES), jnp.float32)

    def sends(ref, position, peers, send_sem, recv_sem):
        part = ref.at[position]
        return [
            pltpu.make_async_remote_copy(
                src_ref=part, dst_ref=part, send_sem=send_sem.at[k], recv_sem=recv_sem.at[k],
                device_id=peer, device_id_type=MESH,
            )
            for k, peer in enumerate(peers)
        ]

    loads[0].wait()
    loads[1].wait()
    weights = []
    for k in range(4):
        rate = jnp.full((SUB, LANES), rates_ref[k], jnp.float32)
        weights.append(rate * jnp.full((SUB, LANES), shares_ref[k], jnp.float32) / (1.0 + rate))
    loads[2].wait()
    capacity = cap_ref[...].reshape(16, SUB, LANES)
    storage = 1.0 + capacity * (weights[0] + weights[1] + weights[2] + weights[3])
    storage = storage.reshape(ROWS, LANES)
    sto_ref[...] = storage

    steps = (1, 2, 4)
    loads[3].wait()
    y_face = strided(dy_ref, 16).reshape(8, 2, SUB, LANES)
    y_ground = strided(sto_ref, 16).reshape(8, 2, SUB, LANES)
    y_coef, y_saved = chain_coef(y_face, y_ground)
    y_coef, ys_saved = sub_coef(y_coef, steps)
    for k in range(3):
        for t in range(2):
            pc_ref[yy, pl.ds(2 * k + t, 1), :] = y_coef[k][t, 0:1]

    loads[4].wait()
    work_ref[...] = jnp.transpose(dx_ref[...])
    work2_ref[...] = jnp.transpose(storage)
    x_coef, x_saved = chain_coef(strided(work_ref, 16), strided(work2_ref, 16))
    loads[5].wait()
    loads[6].wait()
    imm = imm_ref[...].reshape(4, 16, SUB, LANES)
    mixed = weights[0] * imm[0] + weights[1] * imm[1] + weights[2] * imm[2] + weights[3] * imm[3]
    source = mobile_ref[...].reshape(16, SUB, LANES) + capacity * mixed
    work_ref[...] = jnp.transpose(source.reshape(ROWS, LANES))
    x_side, x_mid = chain_side(strided(work_ref, 16), x_saved)
    x_coef, xs_saved = sub_coef(x_coef, steps)
    x_side, xs_mid = sub_side(x_side, xs_saved, steps)

    def next_lane(value):
        return roll(value, LANES - 1, 1)

    even = (lax.broadcasted_iota(jnp.int32, (SUB, LANES), 1) & 1) == 0

    def both_lanes(value):
        value = jnp.where(even, value, roll(value, 1, 1))
        return jnp.broadcast_to(value[0:1], (SUB, LANES))

    own_coef, half_factors = join_coef(x_coef, [next_lane(value) for value in x_coef])
    own_side, half_middle = join_side(x_side, [next_lane(value) for value in x_side], half_factors)
    own_coef = [both_lanes(value) for value in own_coef]
    own_side = [both_lanes(value) for value in own_side]
    for k, value in enumerate(own_coef + own_side):
        x_ref[0, pl.ds(k, 1), :] = value[0:1]

    pl.semaphore_wait(barrier, len(entered))

    x_copies = [
        pltpu.make_async_remote_copy(
            src_ref=x_ref.at[0], dst_ref=x_ref.at[XG_SIZE - k], send_sem=x_send.at[k - 1],
            recv_sem=x_recv.at[k - 1], device_id=x_peers[k - 1], device_id_type=MESH,
        )
        for k in range(1, XG_SIZE)
    ]
    pc_copies = sends(pc_ref, yy, y_peers, pc_send, pc_recv)
    for copy in x_copies + pc_copies:
        copy.start()
    for peer in z_near:
        pl.semaphore_signal(ready.at[0], inc=1, device_id=peer, device_id_type=MESH)
    pl.semaphore_wait(ready.at[0], len(z_near))
    for peer in z_twos:
        pl.semaphore_signal(ready.at[1], inc=1, device_id=peer, device_id_type=MESH)

    one = jnp.ones((SUB, LANES), jnp.float32)
    none = jnp.zeros((SUB, LANES), jnp.float32)

    def responses(saved, subs, middles, sub_middles, u_left, u_right, out):
        u_left, u_right = sub_back(subs, sub_middles, steps, u_left, u_right)
        cells = chain_back(saved, middles, u_left, u_right).reshape(16, SUB, LANES)
        for v in range(16):
            out[pl.ds(v, SUB, stride=16), :] = cells[v]
        return out[...]

    no_mid = [None] * len(x_mid)
    no_sub = [None] * len(steps)
    still = responses(x_saved, xs_saved, x_mid, xs_mid, none, none, work_ref)
    by_left = responses(x_saved, xs_saved, no_mid, no_sub, one, none, work2_ref)
    by_right = responses(x_saved, xs_saved, no_mid, no_sub, none, one, res_ref.at[0])
    half_still = both_lanes(half_middle * half_factors[2])[0:1]
    half_before = both_lanes(half_factors[0])[0:1]
    half_last = both_lanes(half_factors[1])[0:1]
    first = even[0:1]
    res_ref[0] = still + jnp.where(first, by_right, by_left) * half_still
    res_ref[1] = jnp.where(first, by_left + by_right * half_before, by_left * half_before)
    res_ref[2] = jnp.where(first, by_right * half_last, by_right + by_left * half_last)

    both = jnp.ones((2, SUB, LANES), jnp.float32)
    neither = jnp.zeros((2, SUB, LANES), jnp.float32)
    no_mid = [None] * len(y_saved)
    res_ref[5] = responses(y_saved, ys_saved, no_mid, no_sub, both, neither, work_ref)
    res_ref[6] = responses(y_saved, ys_saved, no_mid, no_sub, neither, both, work2_ref)
    res_ref[3] = res_ref[5] * sto_ref[...]
    res_ref[4] = res_ref[6] * sto_ref[...]

    for copy in pc_copies:
        copy.wait_recv()

    def group_rows(ref, k):
        flat = ref.reshape(SUB * 8, LANES)
        return jnp.stack([flat[pl.ds(2 * k + t, SUB, stride=8), :] for t in range(2)])

    def spread(value):
        return jnp.broadcast_to(value[:, 0:1], value.shape)

    def at_row(value, place):
        for t in range(2):
            pick_ref[t] = value[t]
        return jnp.stack([pick_ref[t, pl.ds(place, SUB, stride=0), :] for t in range(2)])

    p_steps = (1, 2)
    p_coef, p_saved = sub_coef([group_rows(pc_ref, k) for k in range(3)], p_steps)
    own = xlo * Z_SIZE + zz
    for k in range(3):
        for t in range(2):
            zc_ref[own, pl.ds(2 * k + t, 1), :] = p_coef[k][t, 0:1]
    zc_part = zc_ref.at[own, pl.ds(0, 6)]
    zc_places = [yd - zz * Y_SIZE + jnp.where(zz <= k, k + 1, k) * Y_SIZE for k in range(Z_SIZE - 1)]
    zc_places += [yd + across + z_turns[k] for k in (0, 1, 7, 2, 6, 3, 5, 4)]
    zc_copies = [
        pltpu.make_async_remote_copy(
            src_ref=zc_part, dst_ref=zc_part, send_sem=zc_send, recv_sem=zc_recv,
            device_id={"xg": xg, "yd": place}, device_id_type=MESH,
        )
        for place in zc_places
    ]
    for copy in zc_copies[:4] + zc_copies[7:-3]:
        copy.start()

    place = lax.broadcasted_iota(jnp.int32, (2, SUB, LANES), 1)
    unit = jnp.where(place == yy, 1.0, 0.0)
    zero = jnp.zeros_like(unit)
    from_left, _ = sub_side((unit, zero), p_saved, p_steps)
    from_right, _ = sub_side((zero, unit), p_saved, p_steps)
    row = lax.broadcasted_iota(jnp.int32, (SUB, LANES), 0)

    def in_rows(pair):
        (a, b), (c, d) = [spread(value) for value in pair]
        return jnp.where(row == 0, a, jnp.where(row == 1, b, jnp.where(row == 2, c, d)))

    from_left = in_rows(from_left)
    from_right = in_rows(from_right)

    for copy in x_copies:
        copy.wait_recv()

    def block(g):
        rows = [jnp.broadcast_to(x_ref[g, pl.ds(k, 1), :], (SUB, LANES)) for k in range(5)]
        return rows[:3], rows[3:]

    rest_coef, rest_side = block(1)
    for g in (2, 3):
        coef, side = block(g)
        rest_coef, factors = join_coef(rest_coef, coef)
        rest_side, _ = join_side(rest_side, side, factors)
    u_before, u_last = ring_solve(ring_coef(own_coef, rest_coef), own_side, rest_side)
    after_x = jnp.transpose(res_ref[0] + res_ref[1] * u_before[0:1] + res_ref[2] * u_last[0:1])

    def total(weights):
        terms = (weights * after_x).reshape(16, SUB, LANES)
        while terms.shape[0] > 1:
            low, high = halves(terms)
            terms = low + high
        terms = terms[0] + roll(terms[0], 4, 0)
        return terms + roll(terms, 2, 0)

    f_left, f_right = total(res_ref[3]), total(res_ref[4])
    part_ref[...] = (from_left * f_left + from_right * f_right)[0:4]
    pr_ref[yy] = jnp.where(row < 2, f_left, f_right)
    pr_copies = sends(pr_ref, yy, y_peers, pr_send, pr_recv)
    part_copies = [
        pltpu.make_async_remote_copy(
            src_ref=part_ref, dst_ref=parts_ref.at[yd], send_sem=part_send, recv_sem=part_recv,
            device_id={"xg": xg, "yd": starts[k] + y}, device_id_type=MESH,
        )
        for k, y in sorted(
            ((k, y) for k in range(len(starts)) for y in range(Y_SIZE)),
            key=lambda place: (place[0] // 2 >= 4, 60 * (place[0] // 2) + 75 * min(place[1], 2), place),
        )
    ]
    for copy in pr_copies:
        copy.start()
    pl.semaphore_wait(ready.at[1], len(z_twos))
    for copy in zc_copies[-3:] + part_copies[:32] + zc_copies[4:7]:
        copy.start()
    parts_ref[pl.ds(yd - yy, Y_SIZE)] = jnp.zeros((Y_SIZE, 4, LANES), jnp.float32)

    work_ref[...] = after_x * sto_ref[...]
    y_side, y_mid = chain_side(strided(work_ref, 16).reshape(8, 2, SUB, LANES), y_saved)
    _, ys_mid = sub_side(y_side, ys_saved, steps)
    res_ref[7] = responses(y_saved, ys_saved, y_mid, ys_mid, neither, neither, work2_ref)

    def z_rows(ref, half, k):
        flat = ref.reshape(ref.shape[0] * 8, LANES)
        return jnp.stack(
            [
                jnp.stack([flat[pl.ds(half * h + 2 * k + t, Z_SIZE, stride=8), :] for t in range(2)])
                for h in range(2)
            ]
        )

    for copy in pr_copies:
        copy.wait_recv()
    for copy in part_copies[32:]:
        copy.start()
    p_side, p_mid = sub_side([group_rows(pr_ref, k) for k in range(2)], p_saved, p_steps)
    other_coef = zc_ref.at[pl.ds(0, len(zc_copies)), pl.ds(0, 6)]
    pltpu.make_async_copy(other_coef, other_coef, zc_recv).wait()

    z_coef, z_saved = sub_coef([z_rows(zc_ref, 8 * Z_SIZE, k) for k in range(3)], steps)
    z_ring = ring_coef([value[0] for value in z_coef], [value[1] for value in z_coef])


    others = parts_ref.at[pl.ds(0, len(part_copies))]
    pltpu.make_async_copy(others, others, part_recv).wait()
    for h in range(2):
        for z in range(Z_SIZE):
            first = h * (Z_SIZE * Y_SIZE) + z * Y_SIZE
            total = parts_ref[first] + parts_ref[first + 1] + (parts_ref[first + 2] + parts_ref[first + 3])
            sums_ref[z, 4 * h : 4 * h + 4, :] = total
    for k in range(2):
        for t in range(2):
            sums_ref[zz, pl.ds(4 * xlo + 2 * k + t, 1), :] = p_side[k][t, 0:1]
    z_side, z_mid = sub_side([z_rows(sums_ref, 4, k) for k in range(2)], z_saved, steps)
    u_p, u_q = ring_solve(z_ring, [value[0] for value in z_side], [value[1] for value in z_side])

    lower = xlo == 0
    u_p, u_q = spread(u_p), spread(u_q)
    u_left, u_right = jnp.where(lower, u_p, u_q), jnp.where(lower, u_q, u_p)
    own_saved = [tuple(jnp.where(lower, value[0], value[1]) for value in factors) for factors in z_saved]
    own_mid = [jnp.where(lower, value[0], value[1]) for value in z_mid]
    u_left, u_right = sub_back(own_saved, own_mid, steps, u_left, u_right)
    u_left, u_right = at_row(u_left, zz), at_row(u_right, zz)
    u_left, u_right = sub_back(p_saved, p_mid, p_steps, u_left, u_right)
    u_left, u_right = at_row(u_left, yy), at_row(u_right, yy)
    lower_half = (row & 1) == 0
    u_left = jnp.where(lower_half, u_left[0], u_left[1])
    u_right = jnp.where(lower_half, u_right[0], u_right[1])
    own, by_left, by_right = [res_ref[k].reshape(16, SUB, LANES) for k in (7, 5, 6)]
    out_ref[...] = (own + by_left * u_left + by_right * u_right).reshape(ROWS, LANES)

    for copy in x_copies + pc_copies + pr_copies:
        copy.wait_send()
    pltpu.make_async_copy(other_coef, other_coef, zc_send).wait()
    pltpu.make_async_copy(others, others, part_send).wait()


def local(mobile, dispersion_x, dispersion_y, capacity, immobile, exchange_rates, rate_shares):
    flat = [value.reshape(ROWS, LANES) for value in (mobile, dispersion_x, dispersion_y, capacity)]
    any_spec = pl.BlockSpec(memory_space=pl.ANY)
    square = pltpu.VMEM((ROWS, LANES), jnp.float32)
    zones = pltpu.SMEM((4,), jnp.float32)
    dma = pltpu.SemaphoreType.DMA
    updated = pl.pallas_call(
        kernel,
        out_shape=pltpu.VMEM((ROWS, LANES), jnp.float32),
        in_specs=[any_spec] * 7,
        out_specs=pl.BlockSpec(memory_space=pltpu.VMEM),
        scratch_shapes=[
            square, square, square, square, pltpu.VMEM((4 * ROWS, LANES), jnp.float32), zones, zones,
            square, square, square,
            pltpu.VMEM((XG_SIZE, 8, LANES), jnp.float32),
            pltpu.VMEM((SUB, 8, LANES), jnp.float32),
            pltpu.VMEM((SUB, 8, LANES), jnp.float32),
            pltpu.VMEM((XLO_SIZE * Z_SIZE, 8, LANES), jnp.float32),
            pltpu.VMEM((4, LANES), jnp.float32),
            pltpu.VMEM((PLANE * Z_SIZE, 4, LANES), jnp.float32),
            pltpu.VMEM((Z_SIZE, 8, LANES), jnp.float32),
            pltpu.VMEM((2, SUB, LANES), jnp.float32),
            pltpu.VMEM((8, ROWS, LANES), jnp.float32),
            dma((7,)),
            dma((XG_SIZE - 1,)), dma((XG_SIZE - 1,)),
            dma((Y_SIZE - 1,)), dma((Y_SIZE - 1,)), dma((Y_SIZE - 1,)), dma((Y_SIZE - 1,)),
            dma(()), dma(()), dma(()), dma(()),
            pltpu.SemaphoreType.REGULAR((2,)),
        ],
        compiler_params=pltpu.CompilerParams(collective_id=0, has_side_effects=True),
    )(*flat, immobile.reshape(4 * ROWS, LANES), exchange_rates, rate_shares)
    return updated.reshape(mobile.shape)


def solution(mesh):
    return jax.shard_map(
        local,
        mesh=mesh,
        in_specs=(
            P("yd", None, "xg"),
            P("yd", None, "xg"),
            P("yd", None, "xg"),
            P("yd", None, "xg"),
            P(None, "yd", None, "xg"),
            P(),
            P(),
        ),
        out_specs=P("yd", None, "xg"),
        check_vma=False,
    )
```

```python
import functools

import jax
import jax.numpy as jnp
from jax import lax
from jax.experimental import pallas as pl
from jax.experimental.pallas import tpu as pltpu
from jax.sharding import PartitionSpec as P

MESH = pl.DeviceIdType.MESH
Y_SIZE, Z_SIZE, XLO_SIZE, XG_SIZE = 4, 8, 2, 4
PLANE = XLO_SIZE * Y_SIZE
ROWS = 128
LANES = 128
SUB = 8

roll = pltpu.roll


def join_coef(left, right):
    e_a, gl_a, gr_a = left
    e_b, gl_b, gr_b = right
    ground = gr_a + gl_b
    inverse = 1.0 / (ground + (e_a + e_b))
    a = e_a * inverse
    b = e_b * inverse
    return (e_a * b, gl_a + a * ground, gr_b + b * ground), (a, b, inverse)


def join_side(left, right, factors):
    a, b, _ = factors
    middle = left[1] + right[0]
    return (left[0] + a * middle, right[1] + b * middle), middle


def between(factors, middle, u_left, u_right):
    a, b, inverse = factors
    carried = a * u_left + b * u_right
    return carried if middle is None else middle * inverse + carried


def halves(values):
    count = values.shape[0]
    pairs = values.reshape((count // 2, 2) + values.shape[1:])
    return pairs[:, 0], pairs[:, 1]


def woven(first, second):
    count = first.shape[0]
    return jnp.stack([first, second], axis=1).reshape((2 * count,) + first.shape[1:])


def chain_coef(face, ground):
    (e_a, e_b), (g_a, g_b) = halves(face), halves(ground)
    inverse = 1.0 / (g_a + (e_a + e_b))
    a = e_a * inverse
    b = e_b * inverse
    coef = (e_a * b, a * g_a, g_b + b * g_a)
    saved = [(a, b, inverse)]
    while coef[0].shape[0] > 1:
        split = [halves(value) for value in coef]
        coef, factors = join_coef([s[0] for s in split], [s[1] for s in split])
        saved.append(factors)
    return tuple(value[0] for value in coef), saved


def chain_side(source, saved):
    f_a, f_b = halves(source)
    a, b, _ = saved[0]
    side = (a * f_a, f_b + b * f_a)
    middles = [f_a]
    for factors in saved[1:]:
        split = [halves(value) for value in side]
        side, middle = join_side([s[0] for s in split], [s[1] for s in split], factors)
        middles.append(middle)
    return tuple(value[0] for value in side), middles


def chain_back(saved, middles, u_left, u_right):
    u_left, u_right = u_left[None], u_right[None]
    for level in reversed(range(len(saved))):
        u_mid = between(saved[level], middles[level], u_left, u_right)
        if level:
            u_left, u_right = woven(u_left, u_mid), woven(u_mid, u_right)
        else:
            u_right = woven(u_mid, u_right)
    return u_right


def ahead(value, steps):
    return roll(value, value.shape[-2] - steps, value.ndim - 2)


def behind(value, steps):
    return roll(value, steps, value.ndim - 2)


def sub_coef(coef, steps):
    saved = []
    for step in steps:
        coef, factors = join_coef(coef, [ahead(value, step) for value in coef])
        saved.append(factors)
    return coef, saved


def sub_side(side, saved, steps):
    middles = []
    for step, factors in zip(steps, saved):
        side, middle = join_side(side, [ahead(value, step) for value in side], factors)
        middles.append(middle)
    return side, middles


def sub_back(saved, middles, steps, u_left, u_right):
    place = lax.broadcasted_iota(jnp.int32, u_left.shape, u_left.ndim - 2)
    for step, factors, middle in reversed(list(zip(steps, saved, middles))):
        u_mid = between(factors, middle, u_left, u_right)
        first = (place & step) == 0
        u_left, u_right = (
            jnp.where(first, u_left, behind(u_mid, step)),
            jnp.where(first, u_mid, behind(u_right, step)),
        )
    return u_left, u_right


def ring_coef(first, second):
    link = first[0] + second[0]
    ground_q = first[2] + second[1]
    ground_p = second[2] + first[1]
    inverse = 1.0 / (ground_q * ground_p + link * (ground_q + ground_p))
    link = link * inverse
    return link, ground_p * inverse + link, ground_q * inverse + link


def ring_solve(ring, first, second):
    link, to_q, to_p = ring
    f_q = first[1] + second[0]
    f_p = second[1] + first[0]
    return to_p * f_p + link * f_q, to_q * f_q + link * f_p


def strided(ref, stride):
    return jnp.stack([ref[pl.ds(start, SUB, stride=stride), :] for start in range(stride)])


def kernel(
    mobile_hbm, dx_hbm, dy_hbm, cap_hbm, imm_hbm, rates_hbm, shares_hbm, out_ref,
    mobile_ref, dx_ref, dy_ref, cap_ref, imm_ref, rates_ref, shares_ref, sto_ref, work_ref, work2_ref,
    x_ref, pc_ref, pr_ref, zc_ref, part_ref, parts_ref, sums_ref, pick_ref, res_ref,
    in_sem, x_send, x_recv, pc_send, pc_recv, pr_send, pr_recv,
    zc_send, zc_recv, part_send, part_recv, ready,
):
    xg = lax.axis_index("xg")
    yd = lax.axis_index("yd")
    xlo = yd // (Z_SIZE * Y_SIZE)
    zz = (yd // Y_SIZE) % Z_SIZE
    yy = yd % Y_SIZE
    slot = xlo * Y_SIZE + yy

    loads = [
        pltpu.make_async_copy(src, dst, in_sem.at[i])
        for i, (src, dst) in enumerate(
            [
                (rates_hbm, rates_ref), (shares_hbm, shares_ref), (cap_hbm, cap_ref), (dy_hbm, dy_ref),
                (dx_hbm, dx_ref), (imm_hbm, imm_ref), (mobile_hbm, mobile_ref),
            ]
        )
    ]

    def turned(position, steps, size):
        return jnp.where(position >= size - steps, steps - size, steps)

    across = jnp.where(xlo == 0, Z_SIZE * Y_SIZE, -Z_SIZE * Y_SIZE)
    y_turns = [turned(yy, k, Y_SIZE) for k in range(1, Y_SIZE)]
    x_peers = [{"xg": xg + turned(xg, k, XG_SIZE), "yd": yd} for k in range(1, XG_SIZE)]
    y_peers = [{"xg": xg, "yd": yd + turn} for turn in y_turns]
    plane_peers = y_peers + [{"xg": xg, "yd": yd + across + turn} for turn in [0] + y_turns]
    z_turns = [turned(zz, k, Z_SIZE) * Y_SIZE for k in range(Z_SIZE)]
    z_twos = [{"xg": xg, "yd": yd + z_turns[k]} for k in (2, Z_SIZE - 2)]
    z_near = z_twos + [{"xg": xg, "yd": yd + z_turns[k]} for k in (1, Z_SIZE - 1)]
    entered = plane_peers[::-1] + x_peers + z_near
    barrier = pltpu.get_barrier_semaphore()

    @pl.when(yd >= 0)
    def _():
        for peer in entered:
            pl.semaphore_signal(barrier, inc=1, device_id=peer, device_id_type=MESH)

    for load in loads:
        load.start()

    firsts = [h * (Z_SIZE * Y_SIZE) + z * Y_SIZE for z in range(Z_SIZE) for h in range(XLO_SIZE)]
    column = zz * XLO_SIZE + xlo
    starts = [jnp.where(column <= k, firsts[k + 1], firsts[k]) for k in range(len(firsts) - 1)]

    pc_ref[Y_SIZE:] = jnp.ones((Y_SIZE, 8, LANES), jnp.float32)
    pr_ref[Y_SIZE:] = jnp.zeros((Y_SIZE, 8, LANES), jnp.float32)

    def sends(ref, position, peers, send_sem, recv_sem):
        part = ref.at[position]
        return [
            pltpu.make_async_remote_copy(
                src_ref=part, dst_ref=part, send_sem=send_sem.at[k], recv_sem=recv_sem.at[k],
                device_id=peer, device_id_type=MESH,
            )
            for k, peer in enumerate(peers)
        ]

    loads[0].wait()
    loads[1].wait()
    weights = []
    for k in range(4):
        rate = jnp.full((SUB, LANES), rates_ref[k], jnp.float32)
        weights.append(rate * jnp.full((SUB, LANES), shares_ref[k], jnp.float32) / (1.0 + rate))
    loads[2].wait()
    capacity = cap_ref[...].reshape(16, SUB, LANES)
    storage = 1.0 + capacity * (weights[0] + weights[1] + weights[2] + weights[3])
    storage = storage.reshape(ROWS, LANES)
    sto_ref[...] = storage

    steps = (1, 2, 4)
    loads[3].wait()
    y_face = strided(dy_ref, 16).reshape(8, 2, SUB, LANES)
    y_ground = strided(sto_ref, 16).reshape(8, 2, SUB, LANES)
    y_coef, y_saved = chain_coef(y_face, y_ground)
    y_coef, ys_saved = sub_coef(y_coef, steps)
    for k in range(3):
        for t in range(2):
            pc_ref[yy, pl.ds(2 * k + t, 1), :] = y_coef[k][t, 0:1]

    loads[4].wait()
    work_ref[...] = jnp.transpose(dx_ref[...])
    work2_ref[...] = jnp.transpose(storage)
    x_coef, x_saved = chain_coef(strided(work_ref, 16), strided(work2_ref, 16))
    loads[5].wait()
    loads[6].wait()
    imm = imm_ref[...].reshape(4, 16, SUB, LANES)
    mixed = weights[0] * imm[0] + weights[1] * imm[1] + weights[2] * imm[2] + weights[3] * imm[3]
    source = mobile_ref[...].reshape(16, SUB, LANES) + capacity * mixed
    work_ref[...] = jnp.transpose(source.reshape(ROWS, LANES))
    x_side, x_mid = chain_side(strided(work_ref, 16), x_saved)
    x_coef, xs_saved = sub_coef(x_coef, steps)
    x_side, xs_mid = sub_side(x_side, xs_saved, steps)

    def next_lane(value):
        return roll(value, LANES - 1, 1)

    even = (lax.broadcasted_iota(jnp.int32, (SUB, LANES), 1) & 1) == 0

    def both_lanes(value):
        value = jnp.where(even, value, roll(value, 1, 1))
        return jnp.broadcast_to(value[0:1], (SUB, LANES))

    own_coef, half_factors = join_coef(x_coef, [next_lane(value) for value in x_coef])
    own_side, half_middle = join_side(x_side, [next_lane(value) for value in x_side], half_factors)
    own_coef = [both_lanes(value) for value in own_coef]
    own_side = [both_lanes(value) for value in own_side]
    for k, value in enumerate(own_coef + own_side):
        x_ref[0, pl.ds(k, 1), :] = value[0:1]

    pl.semaphore_wait(barrier, len(entered))

    x_copies = [
        pltpu.make_async_remote_copy(
            src_ref=x_ref.at[0], dst_ref=x_ref.at[XG_SIZE - k], send_sem=x_send.at[k - 1],
            recv_sem=x_recv.at[k - 1], device_id=x_peers[k - 1], device_id_type=MESH,
        )
        for k in range(1, XG_SIZE)
    ]
    pc_copies = sends(pc_ref, yy, y_peers, pc_send, pc_recv)
    for copy in x_copies + pc_copies:
        copy.start()
    for peer in z_near:
        pl.semaphore_signal(ready.at[0], inc=1, device_id=peer, device_id_type=MESH)
    pl.semaphore_wait(ready.at[0], len(z_near))
    for peer in z_twos:
        pl.semaphore_signal(ready.at[1], inc=1, device_id=peer, device_id_type=MESH)

    one = jnp.ones((SUB, LANES), jnp.float32)
    none = jnp.zeros((SUB, LANES), jnp.float32)

    def responses(saved, subs, middles, sub_middles, u_left, u_right, out):
        u_left, u_right = sub_back(subs, sub_middles, steps, u_left, u_right)
        cells = chain_back(saved, middles, u_left, u_right).reshape(16, SUB, LANES)
        for v in range(16):
            out[pl.ds(v, SUB, stride=16), :] = cells[v]
        return out[...]

    no_mid = [None] * len(x_mid)
    no_sub = [None] * len(steps)
    still = responses(x_saved, xs_saved, x_mid, xs_mid, none, none, work_ref)
    by_left = responses(x_saved, xs_saved, no_mid, no_sub, one, none, work2_ref)
    by_right = responses(x_saved, xs_saved, no_mid, no_sub, none, one, res_ref.at[0])
    half_still = both_lanes(half_middle * half_factors[2])[0:1]
    half_before = both_lanes(half_factors[0])[0:1]
    half_last = both_lanes(half_factors[1])[0:1]
    first = even[0:1]
    res_ref[0] = still + jnp.where(first, by_right, by_left) * half_still
    res_ref[1] = jnp.where(first, by_left + by_right * half_before, by_left * half_before)
    res_ref[2] = jnp.where(first, by_right * half_last, by_right + by_left * half_last)

    both = jnp.ones((2, SUB, LANES), jnp.float32)
    neither = jnp.zeros((2, SUB, LANES), jnp.float32)
    no_mid = [None] * len(y_saved)
    res_ref[5] = responses(y_saved, ys_saved, no_mid, no_sub, both, neither, work_ref)
    res_ref[6] = responses(y_saved, ys_saved, no_mid, no_sub, neither, both, work2_ref)
    res_ref[3] = res_ref[5] * sto_ref[...]
    res_ref[4] = res_ref[6] * sto_ref[...]

    for copy in pc_copies:
        copy.wait_recv()

    def group_rows(ref, k):
        flat = ref.reshape(SUB * 8, LANES)
        return jnp.stack([flat[pl.ds(2 * k + t, SUB, stride=8), :] for t in range(2)])

    def spread(value):
        return jnp.broadcast_to(value[:, 0:1], value.shape)

    def at_row(value, place):
        for t in range(2):
            pick_ref[t] = value[t]
        return jnp.stack([pick_ref[t, pl.ds(place, SUB, stride=0), :] for t in range(2)])

    p_steps = (1, 2)
    p_coef, p_saved = sub_coef([group_rows(pc_ref, k) for k in range(3)], p_steps)
    own = xlo * Z_SIZE + zz
    for k in range(3):
        for t in range(2):
            zc_ref[own, pl.ds(2 * k + t, 1), :] = p_coef[k][t, 0:1]
    zc_part = zc_ref.at[own, pl.ds(0, 6)]
    zc_places = [yd - zz * Y_SIZE + jnp.where(zz <= k, k + 1, k) * Y_SIZE for k in range(Z_SIZE - 1)]
    zc_places += [yd + across + z_turns[k] for k in (0, 1, 7, 2, 6, 3, 5, 4)]
    zc_copies = [
        pltpu.make_async_remote_copy(
            src_ref=zc_part, dst_ref=zc_part, send_sem=zc_send, recv_sem=zc_recv,
            device_id={"xg": xg, "yd": place}, device_id_type=MESH,
        )
        for place in zc_places
    ]
    for copy in zc_copies[:4] + zc_copies[7:-3]:
        copy.start()

    place = lax.broadcasted_iota(jnp.int32, (2, SUB, LANES), 1)
    unit = jnp.where(place == yy, 1.0, 0.0)
    zero = jnp.zeros_like(unit)
    from_left, _ = sub_side((unit, zero), p_saved, p_steps)
    from_right, _ = sub_side((zero, unit), p_saved, p_steps)
    row = lax.broadcasted_iota(jnp.int32, (SUB, LANES), 0)

    def in_rows(pair):
        (a, b), (c, d) = [spread(value) for value in pair]
        return jnp.where(row == 0, a, jnp.where(row == 1, b, jnp.where(row == 2, c, d)))

    from_left = in_rows(from_left)
    from_right = in_rows(from_right)

    for copy in x_copies:
        copy.wait_recv()

    def block(g):
        rows = [jnp.broadcast_to(x_ref[g, pl.ds(k, 1), :], (SUB, LANES)) for k in range(5)]
        return rows[:3], rows[3:]

    rest_coef, rest_side = block(1)
    for g in (2, 3):
        coef, side = block(g)
        rest_coef, factors = join_coef(rest_coef, coef)
        rest_side, _ = join_side(rest_side, side, factors)
    u_before, u_last = ring_solve(ring_coef(own_coef, rest_coef), own_side, rest_side)
    after_x = jnp.transpose(res_ref[0] + res_ref[1] * u_before[0:1] + res_ref[2] * u_last[0:1])

    def total(weights):
        terms = (weights * after_x).reshape(16, SUB, LANES)
        while terms.shape[0] > 1:
            low, high = halves(terms)
            terms = low + high
        terms = terms[0] + roll(terms[0], 4, 0)
        return terms + roll(terms, 2, 0)

    f_left, f_right = total(res_ref[3]), total(res_ref[4])
    part_ref[...] = (from_left * f_left + from_right * f_right)[0:4]
    pr_ref[yy] = jnp.where(row < 2, f_left, f_right)
    pr_copies = sends(pr_ref, yy, y_peers, pr_send, pr_recv)
    part_copies = [
        pltpu.make_async_remote_copy(
            src_ref=part_ref, dst_ref=parts_ref.at[yd], send_sem=part_send, recv_sem=part_recv,
            device_id={"xg": xg, "yd": starts[k] + y}, device_id_type=MESH,
        )
        for k, y in sorted(
            ((k, y) for k in range(len(starts)) for y in range(Y_SIZE)),
            key=lambda place: (place[0] // 2 >= 4, 40 * (place[0] // 2) + 75 * min(place[1], 2), place),
        )
    ]
    for copy in pr_copies:
        copy.start()
    pl.semaphore_wait(ready.at[1], len(z_twos))
    for copy in zc_copies[-3:] + part_copies[:32] + zc_copies[4:7]:
        copy.start()
    parts_ref[pl.ds(yd - yy, Y_SIZE)] = jnp.zeros((Y_SIZE, 4, LANES), jnp.float32)

    work_ref[...] = after_x * sto_ref[...]
    y_side, y_mid = chain_side(strided(work_ref, 16).reshape(8, 2, SUB, LANES), y_saved)
    _, ys_mid = sub_side(y_side, ys_saved, steps)
    res_ref[7] = responses(y_saved, ys_saved, y_mid, ys_mid, neither, neither, work2_ref)

    def z_rows(ref, half, k):
        flat = ref.reshape(ref.shape[0] * 8, LANES)
        return jnp.stack(
            [
                jnp.stack([flat[pl.ds(half * h + 2 * k + t, Z_SIZE, stride=8), :] for t in range(2)])
                for h in range(2)
            ]
        )

    for copy in pr_copies:
        copy.wait_recv()
    for copy in part_copies[32:]:
        copy.start()
    p_side, p_mid = sub_side([group_rows(pr_ref, k) for k in range(2)], p_saved, p_steps)
    other_coef = zc_ref.at[pl.ds(0, len(zc_copies)), pl.ds(0, 6)]
    pltpu.make_async_copy(other_coef, other_coef, zc_recv).wait()

    z_coef, z_saved = sub_coef([z_rows(zc_ref, 8 * Z_SIZE, k) for k in range(3)], steps)
    z_ring = ring_coef([value[0] for value in z_coef], [value[1] for value in z_coef])


    others = parts_ref.at[pl.ds(0, len(part_copies))]
    pltpu.make_async_copy(others, others, part_recv).wait()
    for h in range(2):
        for z in range(Z_SIZE):
            first = h * (Z_SIZE * Y_SIZE) + z * Y_SIZE
            total = parts_ref[first] + parts_ref[first + 1] + (parts_ref[first + 2] + parts_ref[first + 3])
            sums_ref[z, 4 * h : 4 * h + 4, :] = total
    for k in range(2):
        for t in range(2):
            sums_ref[zz, pl.ds(4 * xlo + 2 * k + t, 1), :] = p_side[k][t, 0:1]
    z_side, z_mid = sub_side([z_rows(sums_ref, 4, k) for k in range(2)], z_saved, steps)
    u_p, u_q = ring_solve(z_ring, [value[0] for value in z_side], [value[1] for value in z_side])

    lower = xlo == 0
    u_p, u_q = spread(u_p), spread(u_q)
    u_left, u_right = jnp.where(lower, u_p, u_q), jnp.where(lower, u_q, u_p)
    own_saved = [tuple(jnp.where(lower, value[0], value[1]) for value in factors) for factors in z_saved]
    own_mid = [jnp.where(lower, value[0], value[1]) for value in z_mid]
    u_left, u_right = sub_back(own_saved, own_mid, steps, u_left, u_right)
    u_left, u_right = at_row(u_left, zz), at_row(u_right, zz)
    u_left, u_right = sub_back(p_saved, p_mid, p_steps, u_left, u_right)
    u_left, u_right = at_row(u_left, yy), at_row(u_right, yy)
    lower_half = (row & 1) == 0
    u_left = jnp.where(lower_half, u_left[0], u_left[1])
    u_right = jnp.where(lower_half, u_right[0], u_right[1])
    own, by_left, by_right = [res_ref[k].reshape(16, SUB, LANES) for k in (7, 5, 6)]
    out_ref[...] = (own + by_left * u_left + by_right * u_right).reshape(ROWS, LANES)

    for copy in x_copies + pc_copies + pr_copies:
        copy.wait_send()
    pltpu.make_async_copy(other_coef, other_coef, zc_send).wait()
    pltpu.make_async_copy(others, others, part_send).wait()


def local(mobile, dispersion_x, dispersion_y, capacity, immobile, exchange_rates, rate_shares):
    flat = [value.reshape(ROWS, LANES) for value in (mobile, dispersion_x, dispersion_y, capacity)]
    any_spec = pl.BlockSpec(memory_space=pl.ANY)
    square = pltpu.VMEM((ROWS, LANES), jnp.float32)
    zones = pltpu.SMEM((4,), jnp.float32)
    dma = pltpu.SemaphoreType.DMA
    updated = pl.pallas_call(
        kernel,
        out_shape=pltpu.VMEM((ROWS, LANES), jnp.float32),
        in_specs=[any_spec] * 7,
        out_specs=pl.BlockSpec(memory_space=pltpu.VMEM),
        scratch_shapes=[
            square, square, square, square, pltpu.VMEM((4 * ROWS, LANES), jnp.float32), zones, zones,
            square, square, square,
            pltpu.VMEM((XG_SIZE, 8, LANES), jnp.float32),
            pltpu.VMEM((SUB, 8, LANES), jnp.float32),
            pltpu.VMEM((SUB, 8, LANES), jnp.float32),
            pltpu.VMEM((XLO_SIZE * Z_SIZE, 8, LANES), jnp.float32),
            pltpu.VMEM((4, LANES), jnp.float32),
            pltpu.VMEM((PLANE * Z_SIZE, 4, LANES), jnp.float32),
            pltpu.VMEM((Z_SIZE, 8, LANES), jnp.float32),
            pltpu.VMEM((2, SUB, LANES), jnp.float32),
            pltpu.VMEM((8, ROWS, LANES), jnp.float32),
            dma((7,)),
            dma((XG_SIZE - 1,)), dma((XG_SIZE - 1,)),
            dma((Y_SIZE - 1,)), dma((Y_SIZE - 1,)), dma((Y_SIZE - 1,)), dma((Y_SIZE - 1,)),
            dma(()), dma(()), dma(()), dma(()),
            pltpu.SemaphoreType.REGULAR((2,)),
        ],
        compiler_params=pltpu.CompilerParams(collective_id=0, has_side_effects=True),
    )(*flat, immobile.reshape(4 * ROWS, LANES), exchange_rates, rate_shares)
    return updated.reshape(mobile.shape)


def solution(mesh):
    return jax.shard_map(
        local,
        mesh=mesh,
        in_specs=(
            P("yd", None, "xg"),
            P("yd", None, "xg"),
            P("yd", None, "xg"),
            P("yd", None, "xg"),
            P(None, "yd", None, "xg"),
            P(),
            P(),
        ),
        out_specs=P("yd", None, "xg"),
        check_vma=False,
    )
```
